256 devices in a mesh: rows: 64 (over z, x, core), grp: 4 (over y).
Axes of the slice: x: 4, y: 4, z: 8, core: 2. Of those that a mesh axis runs over, the one named last changes fastest.
Arguments:
- observations: float32 [524288, 512], P(('rows', 'grp')), may hold values from -32 to 32, as said below
- sensor_ids: int32 [524288], P(('rows', 'grp')), may hold values from 0 to 127
- sensor_sigma: float32 [128], replicated, may hold values from 0.3 to 3
- buckets: int32 [524288], P(('rows', 'grp')), may hold values from 0 to 63, as said below
- prior_factor: float32 [512, 512], replicated, may hold values from -0.3 to 3, as said below
Outputs:
- whitened: float32 [524288, 512], P(('rows', 'grp'))
- info_factor: float32 [512, 512], replicated
The draws below stay inside these ranges and needn't reach their ends.
Inputs may be any that keep to these rules, and one draw needn't show every extreme that they name: `buckets`: in each aligned block of 2048 rows every bucket index appears exactly 32 times. `observations`: rows are real-valued without further structure. `prior_factor`: upper triangular with a positive diagonal of at least 0.5.
All inputs are finite; a program needn't handle non-finite values.
Results may differ from the reference program's by a relative error of at most 0.00007.
Values sent between devices are 32-bit elements; how exact they have to be, the bound alone decides.
A program may use at most 128 MiB of HBM per device.

```python
import math
import jax
import jax.numpy as jnp
from jax import lax

STATE = 512
ROWS_DEV = 2048
SENSORS = 128
OBS_ROWS = 524288
BUCKET_ROWS = 32
N_ROWS = 64
N_GRP = 4


def draw_observations(key, part):
    first = jax.random.fold_in(key, 0)
    position = jnp.arange(OBS_ROWS, dtype=jnp.float32) / OBS_ROWS
    ramp = (1.0 + 2.0 * position)[:, None]
    values = jnp.clip(jax.random.normal(first, (OBS_ROWS, STATE), jnp.float32), -6.0, 6.0)
    return values * ramp


def draw_buckets(key, part):
    keys = jax.random.split(key, OBS_ROWS // ROWS_DEV)
    orders = jax.vmap(lambda single: jax.random.permutation(single, ROWS_DEV))(keys)
    return (orders // BUCKET_ROWS).reshape(OBS_ROWS).astype(jnp.int32)


def draw_prior_factor(key, part):
    first, second = jax.random.split(key)
    upper = jnp.clip(jax.random.normal(first, (STATE, STATE), jnp.float32) * 0.05, -0.3, 0.3)
    diagonal = jax.random.uniform(second, (STATE,), jnp.float32, 1.0, 2.0)
    return jnp.triu(upper, 1) + jnp.diag(diagonal)


def place_ends(array, own_key, low, largest):
    index_at = [jax.random.randint(jax.random.fold_in(own_key, axis), (), 0, length) for axis, length in enumerate(array.shape)]
    main_axis = array.shape.index(max(array.shape))
    next_to = index_at[:main_axis] + [(index_at[main_axis] + 1) % array.shape[main_axis]] + index_at[main_axis + 1:]
    return array.at[tuple(index_at)].set(low).at[tuple(next_to)].set(largest)


def setup_inputs(seed: int = 0) -> dict:
    streams_of = jax.random.split(jax.random.key(seed), 6)
    observations = draw_observations(jax.random.fold_in(streams_of[5], 71), 0)
    sensor_ids = place_ends(jax.random.randint(streams_of[1], (OBS_ROWS,), 0, SENSORS), jax.random.fold_in(streams_of[1], 1), 0, SENSORS - 1).astype(jnp.int32)
    sensor_sigma = jnp.clip(jnp.exp(jax.random.uniform(streams_of[2], (SENSORS,), jnp.float32, math.log(0.3), math.log(3.0))), 0.3, 3.0)
    buckets = draw_buckets(jax.random.fold_in(streams_of[5], 71), 0)
    prior_factor = draw_prior_factor(jax.random.fold_in(streams_of[5], 71), 0)
    return dict(observations=observations, sensor_ids=sensor_ids, sensor_sigma=sensor_sigma, buckets=buckets, prior_factor=prior_factor)


def reference(observations, sensor_ids, sensor_sigma, buckets, prior_factor):
    inv_sigma = 1.0 / sensor_sigma
    scaled = observations * inv_sigma[sensor_ids][:, None]
    gram_sum = lax.dot_general(scaled.astype(jnp.float32), scaled.astype(jnp.float32), (((0,), (0,)), ((), ())), precision=lax.Precision.HIGHEST, preferred_element_type=jnp.float32)
    prior_gram = jnp.dot(prior_factor.T.astype(jnp.float32), prior_factor.astype(jnp.float32), precision=lax.Precision.HIGHEST, preferred_element_type=jnp.float32)
    information = prior_gram + gram_sum / jnp.float32(OBS_ROWS)
    lower_part = jnp.linalg.cholesky(information)
    info_factor = lower_part.T
    white = lax.linalg.triangular_solve(info_factor, scaled, left_side=False, lower=False, transpose_a=False)
    devices = OBS_ROWS // ROWS_DEV
    blocks = buckets.reshape(devices, ROWS_DEV)
    onehot = (blocks[:, :, None] == jnp.arange(N_ROWS, dtype=jnp.int32)[None, None, :]).astype(jnp.int32)
    running = jnp.cumsum(onehot, axis=1)
    within = jnp.sum(onehot * running, axis=2) - 1
    device_ids = jnp.arange(devices, dtype=jnp.int32)[:, None]
    source = device_ids // N_GRP
    group = device_ids % N_GRP
    target = (blocks * N_GRP + group) * ROWS_DEV + source * BUCKET_ROWS + within
    whitened = jnp.zeros((OBS_ROWS, STATE), jnp.float32).at[target.reshape(-1).astype(jnp.int32)].set(white)
    return (whitened, info_factor)
```

```python
import functools

import jax
import jax.numpy as jnp
from jax import lax
from jax.experimental import pallas as pl
from jax.experimental.pallas import tpu as pltpu
from jax.sharding import PartitionSpec as P

MESH = pl.DeviceIdType.MESH
F32, BF16, I32 = jnp.float32, jnp.bfloat16, jnp.int32
NZ, NX, NC, NY = 8, 4, 2, 4
STEPS = (4, 1, 7, 3, 5, 2, 6, 0)
PANEL = 128


def iota(shape, dim):
    return lax.broadcasted_iota(I32, shape, dim)


def split(values):
    high = values.astype(BF16)
    return high, (values - high.astype(F32)).astype(BF16)


def dot(left, right, dims=((1,), (0,))):
    return lax.dot_general(left, right, (dims, ((), ())), preferred_element_type=F32)


def exact_dot(left, right, dims=((1,), (0,))):
    return lax.dot_general(
        left, right, (dims, ((), ())), precision=lax.Precision.HIGHEST, preferred_element_type=F32
    )


def factor_panel(block):
    tiles = PANEL // 8
    lane = iota((8, PANEL), 1)
    sub = iota((8, PANEL), 0)
    rows = [block[8 * q : 8 * q + 8] for q in range(tiles)]
    invs = [jnp.where(lane == sub + 8 * q, jnp.float32(1.0), jnp.float32(0.0)) for q in range(tiles)]
    for j in range(PANEL):
        p, k = j // 8, j % 8
        pivot_row = rows[p][k : k + 1]
        inv_row = invs[p][k : k + 1]
        root = lax.rsqrt(pivot_row[:, j : j + 1])
        unit_row, unit_inv = pivot_row * root, inv_row * root
        for q in range(p, tiles):
            column = rows[q][:, j : j + 1] * root
            if q == p:
                below = sub > k
                here = sub == k
                new_rows = rows[q] - column * unit_row
                new_invs = invs[q] - column * unit_inv
                rows[q] = jnp.where(below, new_rows, jnp.where(here, unit_row, rows[q]))
                invs[q] = jnp.where(below, new_invs, jnp.where(here, unit_inv, invs[q]))
            else:
                rows[q] = rows[q] - column * unit_row
                invs[q] = invs[q] - column * unit_inv
    return jnp.concatenate(rows, axis=0), jnp.concatenate(invs, axis=0)


def kernel(
    total_rows,
    x_hbm, ids_ref, sigma_ref, buckets_ref, prior_ref,
    out_ref, factor_ref,
    x_buf, high_ref, low_ref, pick_ref, target_ref, scale_ref, sorted_ref, recv_ref,
    gram_ref, pair_ref, half_ref, plane_ref, tiles_ref, line_ref, gather_ref, info_ref, inv_ref, prior_gram_ref,
    inv_high_ref, inv_low_ref,
    x_sem, send_sem, recv_sem, pair_sem, plane_sem, line_sem, line_back_sem, plane_back_sem, pair_back_sem,
):
    me, y = lax.axis_index("rows"), lax.axis_index("grp")
    z, x, c = me // (NX * NC), (me // NC) % NX, me % NC
    rows_dev, state = x_hbm.shape
    groups, per_group = NX * NC, NZ
    block = rows_dev // (NZ * NX * NC)
    chunk = block * per_group

    def row_index(dz, dx, dc):
        return (((z + dz) % NZ) * NX + (x + dx) % NX) * NC + (c + dc) % NC

    loads = []
    for g in range(groups):
        part = pl.ds(g * chunk, chunk)
        copy = pltpu.make_async_copy(x_hbm.at[part], x_buf.at[part], x_sem.at[g])
        copy.start()
        loads.append(copy)

    barrier = pltpu.get_barrier_semaphore()
    for dz in range(NZ):
        for dx in range(NX):
            for dc in range(NC):
                if (dz, dx, dc) != (0, 0, 0):
                    pl.semaphore_signal(
                        barrier, inc=1, device_id={"rows": row_index(dz, dx, dc)}, device_id_type=MESH
                    )
    for dx in range(NX):
        for dy in range(1, NY):
            peer = {"rows": row_index(0, dx, 0), "grp": (y + dy) % NY}
            pl.semaphore_signal(barrier, inc=1, device_id=peer, device_id_type=MESH)

    n_buckets, n_chunks = NZ * NX * NC, rows_dev // 128
    below = (iota((128, 256), 0) <= iota((128, 256), 1)) | (iota((128, 256), 1) >= 128)
    counter = jnp.where(below, jnp.float32(1.0), jnp.float32(0.0)).astype(BF16)
    bucket_no = iota((n_buckets, 128), 0)
    base = jnp.zeros((n_buckets, 128), F32)
    for q in range(n_chunks):
        match = bucket_no == buckets_ref[q : q + 1, :]
        onehot = jnp.where(match, jnp.float32(1.0), jnp.float32(0.0))
        counts = dot(onehot.astype(BF16), counter)
        rank = counts[:, :128] + base
        base = base + counts[:, 128:]
        spot = jnp.where(match, rank.astype(I32) + (bucket_no * block - 1), 0)
        target_ref[:, 128 * q : 128 * q + 128] = jnp.broadcast_to(
            jnp.sum(spot, axis=0, keepdims=True), (8, 128)
        )

    weights = jnp.broadcast_to(1.0 / sigma_ref[...], (128, 128)).T
    w_high, w_mid = split(weights)
    w_low = (weights - w_high.astype(F32) - w_mid.astype(F32)).astype(BF16)
    sensor_no = iota((128, 128), 0)
    for q in range(n_chunks):
        onehot = jnp.where(sensor_no == ids_ref[q : q + 1, :], jnp.float32(1.0), jnp.float32(0.0)).T.astype(BF16)
        scale_ref[128 * q : 128 * q + 128, :] = (
            dot(onehot, w_high) + dot(onehot, w_mid) + dot(onehot, w_low)
        )

    @pl.loop(0, groups)
    def _(g):
        part = pl.ds(pl.multiple_of(g * chunk, chunk), chunk)
        pltpu.make_async_copy(x_hbm.at[part], x_buf.at[part], x_sem.at[g]).wait()
        scale = scale_ref[part, :]
        for n in range(state // 128):
            cols = slice(128 * n, 128 * n + 128)
            high, low = split(x_buf[part, cols] * scale)
            high_ref[part, cols] = high
            low_ref[part, cols] = low

    pl.semaphore_wait(barrier, NZ * NX * NC - 1 + NX * (NY - 1))

    def offsets(g, j):
        return STEPS[j], (g // NC + j) % NX, g % NC

    def is_own(g, j):
        dz, dx, dc = offsets(g, j)
        return (dz == 0) & (dx == 0) & (dc == 0)

    def row_copy(g, j):
        spot = pl.ds(pl.multiple_of(g * chunk + j * block, block), block)
        return pltpu.make_async_remote_copy(
            sorted_ref.at[spot], recv_ref.at[spot],
            send_sem.at[g * per_group + j], recv_sem.at[g * per_group + j],
            device_id={"rows": row_index(*offsets(g, j))}, device_id_type=MESH,
        )

    def sort_and_send(g):
        for j in range(per_group):
            first = row_index(*offsets(g, j)) * block
            for i in range(block // 8):
                hit = target_ref[...] == iota((8, rows_dev), 0) + (first + 8 * i)
                pick_ref[j * block + 8 * i : j * block + 8 * i + 8, :] = jnp.where(
                    hit, jnp.float32(1.0), jnp.float32(0.0)
                ).astype(BF16)
        part = pl.ds(pl.multiple_of(g * chunk, chunk), chunk)
        pick = pick_ref[...]
        sorted_ref[part, :] = dot(pick, high_ref[...]) + dot(pick, low_ref[...])
        for j in range(per_group):
            if STEPS[j] == 0:
                own = is_own(g, j)
                spot = pl.ds(pl.multiple_of(g * chunk + j * block, block), block)

                @pl.when(own)
                def _():
                    recv_ref[spot, :] = sorted_ref[spot, :]

                @pl.when(jnp.logical_not(own))
                def _():
                    row_copy(g, j).start()
            else:
                row_copy(g, j).start()

    def sort_groups(first, last):
        @pl.loop(first, last)
        def _(g):
            sort_and_send(g)

    sort_groups(0, 1)

    gram_ref[...] = jnp.zeros_like(gram_ref)

    @pl.loop(0, groups)
    def _(g):
        part = pl.ds(pl.multiple_of(g * chunk, chunk), chunk)
        high, low = high_ref[part, :], low_ref[part, :]
        along = ((0,), (0,))
        gram_ref[...] += dot(high, high, along) + dot(high, low, along) + dot(low, high, along)

    half_rows = state // NC
    piece_rows = half_rows // (NX * NY)
    mine_half = pl.ds(pl.multiple_of(c * half_rows, half_rows), half_rows)
    other_half = pl.ds(pl.multiple_of((1 - c) * half_rows, half_rows), half_rows)
    partner = {"rows": row_index(0, 0, 1)}
    pair = pltpu.make_async_remote_copy(
        gram_ref.at[other_half], pair_ref, pair_sem.at[0], pair_sem.at[1], device_id=partner, device_id_type=MESH
    )
    pair.start()

    prior = prior_ref[...]
    prior_gram_ref[...] = exact_dot(prior, prior, ((0,), (0,)))
    sort_groups(1, 2)
    pair.wait_recv()
    half_ref[...] = gram_ref[mine_half, :] + pair_ref[...]

    def piece(px, py):
        return pl.ds(pl.multiple_of((px * NY + py) * piece_rows, piece_rows), piece_rows)

    plane = [(dx, dy) for dx in range(NX) for dy in range(NY) if (dx, dy) != (0, 0)]
    plane_copies = []
    for n, (dx, dy) in enumerate(plane):
        px, py = (x + dx) % NX, (y + dy) % NY
        copy = pltpu.make_async_remote_copy(
            half_ref.at[piece(px, py)], plane_ref.at[n], plane_sem.at[0, n], plane_sem.at[1, n],
            device_id={"rows": row_index(0, dx, 0), "grp": py}, device_id_type=MESH,
        )
        copy.start()
        plane_copies.append(copy)
    sort_groups(2, 4)
    for copy in plane_copies:
        copy.wait_recv()
    total = half_ref[piece(x, y), :]
    for n in range(len(plane)):
        total = total + plane_ref[n]
    for t in range(NZ):
        tiles_ref[t] = total[8 * (t // 4) : 8 * (t // 4) + 8, 128 * (t % 4) : 128 * (t % 4) + 128]
    line_copies = []
    for dz in range(1, NZ):
        copy = pltpu.make_async_remote_copy(
            tiles_ref.at[(z + dz) % NZ], line_ref.at[dz], line_sem.at[0, dz], line_sem.at[1, dz],
            device_id={"rows": row_index(dz, 0, 0)}, device_id_type=MESH,
        )
        copy.start()
        line_copies.append(copy)
    sort_groups(4, 6)
    for copy in line_copies:
        copy.wait_recv()
    done = tiles_ref[z]
    for dz in range(1, NZ):
        done = done + line_ref[dz]
    gather_ref[z] = done
    back_copies = []
    for dz in range(1, NZ):
        copy = pltpu.make_async_remote_copy(
            gather_ref.at[z], gather_ref.at[z], line_back_sem.at[0, dz], line_back_sem.at[1, dz],
            device_id={"rows": row_index(dz, 0, 0)}, device_id_type=MESH,
        )
        copy.start()
        back_copies.append(copy)
    sort_groups(6, 8)
    for copy in back_copies:
        copy.wait_recv()
    own_piece = pl.ds(
        pl.multiple_of(c * half_rows + (x * NY + y) * piece_rows, piece_rows), piece_rows
    )
    info_ref[own_piece, :] = jnp.concatenate(
        [jnp.concatenate([gather_ref[4 * a + b] for b in range(4)], axis=1) for a in range(2)], axis=0
    )
    plane_back = []
    for n, (dx, dy) in enumerate(plane):
        copy = pltpu.make_async_remote_copy(
            info_ref.at[own_piece], info_ref.at[own_piece], plane_back_sem.at[0, n], plane_back_sem.at[1, n],
            device_id={"rows": row_index(0, dx, 0), "grp": (y + dy) % NY}, device_id_type=MESH,
        )
        copy.start()
        plane_back.append(copy)
    for copy in plane_back:
        copy.wait_recv()
    pair_back = pltpu.make_async_remote_copy(
        info_ref.at[mine_half], info_ref.at[mine_half], pair_back_sem.at[0], pair_back_sem.at[1],
        device_id=partner, device_id_type=MESH,
    )
    pair_back.start()
    for copies in ([pair], plane_copies, line_copies, back_copies, plane_back):
        for copy in copies:
            copy.wait_send()
    pair_back.wait()

    gram_ref[...] = prior_gram_ref[...] + info_ref[...] / jnp.float32(total_rows)
    inv_ref[...] = jnp.where(iota((state, state), 0) == iota((state, state), 1), jnp.float32(1.0), jnp.float32(0.0))

    @pl.loop(0, state // PANEL)
    def _(k):
        part = pl.ds(pl.multiple_of(k * PANEL, PANEL), PANEL)
        upper, inverse = factor_panel(gram_ref[part, part])
        del upper
        wide = exact_dot(inverse, gram_ref[part, :])
        wide_inv = exact_dot(inverse, inv_ref[part, :])
        row_no = k * PANEL + iota((PANEL, state), 0)
        col_no = iota((PANEL, state), 1)
        wide = jnp.where(col_no >= row_no, wide, jnp.float32(0.0))
        factor_ref[part, :] = wide
        inv_ref[part, :] = wide_inv
        rest = jnp.where(col_no >= (k + 1) * PANEL, wide, jnp.float32(0.0))
        gram_ref[...] = gram_ref[...] - exact_dot(rest, wide, ((0,), (0,)))
        inv_ref[...] = inv_ref[...] - exact_dot(rest, wide_inv, ((0,), (0,)))

    inv_high_ref[...], inv_low_ref[...] = split(inv_ref[...])

    @pl.loop(0, groups)
    def _(g):
        for j in range(per_group):
            if STEPS[j] == 0:
                @pl.when(jnp.logical_not(is_own(g, j)))
                def _():
                    row_copy(g, j).wait()
            else:
                row_copy(g, j).wait()
        part = pl.ds(pl.multiple_of(g * chunk, chunk), chunk)
        high, low = split(recv_ref[part, :])
        inv_high, inv_low = inv_high_ref[...], inv_low_ref[...]
        cross = ((1,), (1,))
        white = dot(high, inv_high, cross) + dot(high, inv_low, cross) + dot(low, inv_high, cross)
        for j in range(per_group):
            dz, dx, dc = offsets(g, j)
            source = row_index(NZ - dz, NX - dx, NC - dc)
            spot = pl.ds(pl.multiple_of(source * block, block), block)
            out_ref[spot, :] = white[j * block : (j + 1) * block]


def shards(observations, sensor_ids, sensor_sigma, buckets, prior_factor):
    rows_dev, state = observations.shape
    total_rows = rows_dev * lax.axis_size(("rows", "grp"))
    vmem = pl.BlockSpec(memory_space=pltpu.VMEM)
    half = state // NC
    piece = half // (NX * NY)
    dma = pltpu.SemaphoreType.DMA
    return pl.pallas_call(
        functools.partial(kernel, total_rows),
        out_shape=(
            jax.ShapeDtypeStruct((rows_dev, state), F32),
            jax.ShapeDtypeStruct((state, state), F32),
        ),
        in_specs=[pl.BlockSpec(memory_space=pl.ANY), vmem, vmem, vmem, vmem],
        out_specs=(vmem, vmem),
        scratch_shapes=[
            pltpu.VMEM((rows_dev, state), F32),
            pltpu.VMEM((rows_dev, state), BF16),
            pltpu.VMEM((rows_dev, state), BF16),
            pltpu.VMEM((rows_dev // (NX * NC), rows_dev), BF16),
            pltpu.VMEM((8, rows_dev), I32),
            pltpu.VMEM((rows_dev, 128), F32),
            pltpu.VMEM((rows_dev, state), F32),
            pltpu.VMEM((rows_dev, state), F32),
            pltpu.VMEM((state, state), F32),
            pltpu.VMEM((half, state), F32),
            pltpu.VMEM((half, state), F32),
            pltpu.VMEM((NX * NY - 1, piece, state), F32),
            pltpu.VMEM((NZ, 8, 128), F32),
            pltpu.VMEM((NZ, 8, 128), F32),
            pltpu.VMEM((NZ, 8, 128), F32),
            pltpu.VMEM((state, state), F32),
            pltpu.VMEM((state, state), F32),
            pltpu.VMEM((state, state), F32),
            pltpu.VMEM((state, state), BF16),
            pltpu.VMEM((state, state), BF16),
            dma((NX * NC,)),
            dma((NZ * NX * NC,)),
            dma((NZ * NX * NC,)),
            dma((2,)),
            dma((2, NX * NY - 1)),
            dma((2, NZ)),
            dma((2, NZ)),
            dma((2, NX * NY - 1)),
            dma((2,)),
        ],
        compiler_params=pltpu.CompilerParams(
            collective_id=0, has_side_effects=True, vmem_limit_bytes=48 << 20
        ),
    )(
        observations,
        sensor_ids.reshape(-1, 128),
        sensor_sigma.reshape(1, -1),
        buckets.reshape(-1, 128),
        prior_factor,
    )


def solution(mesh):
    in_specs = (P(("rows", "grp"), None), P(("rows", "grp")), P(), P(("rows", "grp")), P())
    out_specs = (P(("rows", "grp"), None), P())
    return jax.shard_map(shards, mesh=mesh, in_specs=in_specs, out_specs=out_specs, check_vma=False)
```

```python
import functools

import jax
import jax.numpy as jnp
from jax import lax
from jax.experimental import pallas as pl
from jax.experimental.pallas import tpu as pltpu
from jax.sharding import PartitionSpec as P

MESH = pl.DeviceIdType.MESH
F32, BF16, I32 = jnp.float32, jnp.bfloat16, jnp.int32
NZ, NX, NC, NY = 8, 4, 2, 4
STEPS = (4, 1, 7, 3, 5, 2, 6, 0)
PANEL = 128


def iota(shape, dim):
    return lax.broadcasted_iota(I32, shape, dim)


def split(values):
    high = values.astype(BF16)
    return high, (values - high.astype(F32)).astype(BF16)


def dot(left, right, dims=((1,), (0,))):
    return lax.dot_general(left, right, (dims, ((), ())), preferred_element_type=F32)


def exact_dot(left, right, dims=((1,), (0,))):
    return lax.dot_general(
        left, right, (dims, ((), ())), precision=lax.Precision.HIGHEST, preferred_element_type=F32
    )


def along(piece):
    return jnp.broadcast_to(piece, (8, PANEL))


def root_of(value):
    root = lax.rsqrt(value)
    return root, root * root


def inverse_panel(block):
    tiles = PANEL // 8
    lane, sub = iota((8, PANEL), 1), iota((8, PANEL), 0)
    zero = jnp.float32(0.0)
    rows = [block[8 * q : 8 * q + 8] for q in range(tiles)]
    invs = [jnp.where(lane == sub + 8 * q, jnp.float32(1.0), zero) for q in range(tiles)]
    outs = []
    for p in range(tiles):
        scale = jnp.zeros((8, PANEL), F32)
        for k in (0, 4):
            cols = {
                q: [along(rows[q][:, 8 * p + k + n : 8 * p + k + n + 1]) for n in range(4)] for q in range(p, tiles)
            }
            m = [[along(cols[p][n][k + i : k + i + 1]) for n in range(4)] for i in range(4)]
            a, b, d = m[0][0], m[1][0], m[1][1]
            det = a * d - b * b
            root_a, inv_a = root_of(a)
            root_det, inv_det = root_of(det)
            b02, b03, b12, b13 = m[2][0], m[3][0], m[2][1], m[3][1]
            g02, g12 = (d * b02 - b * b12) * inv_det, (a * b12 - b * b02) * inv_det
            g03, g13 = (d * b03 - b * b13) * inv_det, (a * b13 - b * b03) * inv_det
            s22 = m[2][2] - b02 * g02 - b12 * g12
            s32 = m[3][2] - b03 * g02 - b13 * g12
            s33 = m[3][3] - b03 * g03 - b13 * g13
            low_det = s22 * s33 - s32 * s32
            root_s, inv_s = root_of(s22)
            root_low, inv_low = root_of(low_det)
            f, h = b * inv_a, s32 * inv_s
            for i, root in enumerate((root_a, root_det * (a * root_a), root_s, root_low * (s22 * root_s))):
                scale = jnp.where(sub == k + i, root, scale)

            def eliminate(t0, t1, t2, t3):
                t2 = t2 - g02 * t0 - g12 * t1
                t3 = t3 - g03 * t0 - g13 * t1
                return t0, t1 - f * t0, t2, t3 - h * t2

            weights = (inv_a, a * inv_det, inv_s, s22 * inv_low)
            pivot_rows = eliminate(*(along(rows[p][k + i : k + i + 1]) for i in range(4)))
            pivot_invs = eliminate(*(along(invs[p][k + i : k + i + 1]) for i in range(4)))
            pivot_rows = [value * w for value, w in zip(pivot_rows, weights)]
            pivot_invs = [value * w for value, w in zip(pivot_invs, weights)]
            for q in range(p, tiles):
                x = eliminate(*cols[q])
                if q == p:
                    x = [jnp.where(sub > k + i, x[i], zero) for i in range(4)]
                for held, pivots in ((rows, pivot_rows), (invs, pivot_invs)):
                    held[q] = held[q] - (
                        (x[0] * pivots[0] + x[1] * pivots[1]) + (x[2] * pivots[2] + x[3] * pivots[3])
                    )
        outs.append(invs[p] * scale)
    return jnp.concatenate(outs, axis=0)


def factor_and_invert(matrix_ref, factor_ref, inv_ref):
    state = matrix_ref.shape[0]
    panels = state // PANEL
    factor_ref[...] = jnp.zeros_like(factor_ref)
    down = ((0,), (0,))

    @pl.loop(0, panels)
    def _(k):
        part = pl.ds(pl.multiple_of(k * PANEL, PANEL), PANEL)
        inverse = inverse_panel(matrix_ref[part, part])
        for s in range(panels):

            @pl.when(k == s)
            def _():
                first, last = s * PANEL, (s + 1) * PANEL
                own = slice(first, last)
                wide = exact_dot(inverse, matrix_ref[own, first:])
                keep = iota((PANEL, PANEL), 1) >= iota((PANEL, PANEL), 0)
                factor_ref[own, own] = jnp.where(keep, wide[:, :PANEL], jnp.float32(0.0))
                inv_ref[own, own] = inverse
                if s:
                    inv_ref[own, :first] = exact_dot(inverse, inv_ref[own, :first])
                if s < panels - 1:
                    rest = wide[:, PANEL:]
                    factor_ref[own, last:] = rest
                    inv_ref[own, last:] = jnp.zeros((PANEL, state - last), F32)
                    matrix_ref[last:, last:] = matrix_ref[last:, last:] - exact_dot(rest, rest, down)
                    delta = exact_dot(rest, inv_ref[own, :last], down)
                    if s:
                        inv_ref[last:, :first] = inv_ref[last:, :first] - delta[:, :first]
                    inv_ref[last:, own] = -delta[:, first:]


def kernel(
    total_rows,
    x_hbm, ids_hbm, sigma_hbm, buckets_hbm, prior_hbm,
    out_ref, factor_ref,
    ids_ref, sigma_ref, buckets_ref, prior_ref, x_buf, high_ref, low_ref, pick_ref, target_ref, scale_ref, sorted_ref, recv_ref,
    gram_ref, pair_ref, half_ref, plane_ref, tiles_ref, line_ref, gather_ref, info_ref, inv_ref, prior_gram_ref,
    inv_high_ref, inv_low_ref,
    small_sem, x_sem, send_sem, recv_sem, pair_sem, plane_sem, line_sem, line_back_sem, plane_back_sem, pair_back_sem,
):
    me, y = lax.axis_index("rows"), lax.axis_index("grp")
    z, x, c = me // (NX * NC), (me // NC) % NX, me % NC
    rows_dev, state = x_hbm.shape
    groups, per_group = NX * NC, NZ
    block = rows_dev // (NZ * NX * NC)
    chunk = block * per_group

    def row_index(dz, dx, dc):
        return (((z + dz) % NZ) * NX + (x + dx) % NX) * NC + (c + dc) % NC

    smalls = [
        pltpu.make_async_copy(source, target, small_sem.at[n])
        for n, (source, target) in enumerate(
            ((buckets_hbm, buckets_ref), (ids_hbm, ids_ref), (sigma_hbm, sigma_ref), (prior_hbm, prior_ref))
        )
    ]
    for copy in smalls[:3]:
        copy.start()
    for g in range(groups):
        part = pl.ds(g * chunk, chunk)
        copy = pltpu.make_async_copy(x_hbm.at[part], x_buf.at[part], x_sem.at[g])
        copy.start()
    smalls[3].start()

    barrier = pltpu.get_barrier_semaphore()
    for dz in range(NZ):
        for dx in range(NX):
            for dc in range(NC):
                if (dz, dx, dc) != (0, 0, 0):
                    pl.semaphore_signal(
                        barrier, inc=1, device_id={"rows": row_index(dz, dx, dc)}, device_id_type=MESH
                    )
    for dx in range(NX):
        for dy in range(1, NY):
            peer = {"rows": row_index(0, dx, 0), "grp": (y + dy) % NY}
            pl.semaphore_signal(barrier, inc=1, device_id=peer, device_id_type=MESH)

    smalls[0].wait()

    n_buckets, n_chunks = NZ * NX * NC, rows_dev // 128
    below = (iota((128, 256), 0) <= iota((128, 256), 1)) | (iota((128, 256), 1) >= 128)
    counter = jnp.where(below, jnp.float32(1.0), jnp.float32(0.0)).astype(BF16)
    bucket_no = iota((n_buckets, 128), 0)
    base = jnp.zeros((n_buckets, 128), F32)
    for q in range(n_chunks):
        match = bucket_no == buckets_ref[q : q + 1, :]
        onehot = jnp.where(match, jnp.float32(1.0), jnp.float32(0.0))
        counts = dot(onehot.astype(BF16), counter)
        rank = counts[:, :128] + base
        base = base + counts[:, 128:]
        spot = jnp.where(match, rank.astype(I32) + (bucket_no * block - 1), 0)
        target_ref[:, 128 * q : 128 * q + 128] = jnp.broadcast_to(
            jnp.sum(spot, axis=0, keepdims=True), (8, 128)
        )

    smalls[1].wait()
    smalls[2].wait()

    weights = jnp.broadcast_to(1.0 / sigma_ref[...], (128, 128)).T
    w_high, w_mid = split(weights)
    w_low = (weights - w_high.astype(F32) - w_mid.astype(F32)).astype(BF16)
    sensor_no = iota((128, 128), 0)
    for q in range(n_chunks):
        onehot = jnp.where(sensor_no == ids_ref[q : q + 1, :], jnp.float32(1.0), jnp.float32(0.0)).T.astype(BF16)
        scale_ref[128 * q : 128 * q + 128, :] = (
            dot(onehot, w_high) + dot(onehot, w_mid) + dot(onehot, w_low)
        )

    @pl.loop(0, groups)
    def _(g):
        part = pl.ds(pl.multiple_of(g * chunk, chunk), chunk)
        pltpu.make_async_copy(x_hbm.at[part], x_buf.at[part], x_sem.at[g]).wait()
        scale = scale_ref[part, :]
        for n in range(state // 128):
            cols = slice(128 * n, 128 * n + 128)
            high, low = split(x_buf[part, cols] * scale)
            high_ref[part, cols] = high
            low_ref[part, cols] = low

    pl.semaphore_wait(barrier, NZ * NX * NC - 1 + NX * (NY - 1))

    def offsets(g, j):
        return STEPS[j], (g // NC + j) % NX, g % NC

    def is_own(g, j):
        dz, dx, dc = offsets(g, j)
        return (dz == 0) & (dx == 0) & (dc == 0)

    def row_copy(g, j):
        spot = pl.ds(pl.multiple_of(g * chunk + j * block, block), block)
        return pltpu.make_async_remote_copy(
            sorted_ref.at[spot], recv_ref.at[spot],
            send_sem.at[g * per_group + j], recv_sem.at[g * per_group + j],
            device_id={"rows": row_index(*offsets(g, j))}, device_id_type=MESH,
        )

    def sort(g):
        for j in range(per_group):
            first = row_index(*offsets(g, j)) * block
            for i in range(block // 8):
                hit = target_ref[...] == iota((8, rows_dev), 0) + (first + 8 * i)
                pick_ref[j * block + 8 * i : j * block + 8 * i + 8, :] = jnp.where(
                    hit, jnp.float32(1.0), jnp.float32(0.0)
                ).astype(BF16)
        part = pl.ds(pl.multiple_of(g * chunk, chunk), chunk)
        pick = pick_ref[...]
        sorted_ref[part, :] = dot(pick, high_ref[...]) + dot(pick, low_ref[...])

    def send(g, first=0, last=NZ):
        for j in range(first, last):
            if STEPS[j] == 0:
                own = is_own(g, j)
                spot = pl.ds(pl.multiple_of(g * chunk + j * block, block), block)

                @pl.when(own)
                def _():
                    recv_ref[spot, :] = sorted_ref[spot, :]

                @pl.when(jnp.logical_not(own))
                def _():
                    row_copy(g, j).start()
            else:
                row_copy(g, j).start()

    def sort_group(which):
        @pl.loop(which, which + 1)
        def _(g):
            sort(g)

    def send_group(which, first=0, last=NZ):
        @pl.loop(which, which + 1)
        def _(g):
            send(g, first, last)

    sort_group(0)
    send_group(0)

    gram_ref[...] = jnp.zeros_like(gram_ref)

    @pl.loop(0, groups)
    def _(g):
        part = pl.ds(pl.multiple_of(g * chunk, chunk), chunk)
        high, low = high_ref[part, :], low_ref[part, :]
        along = ((0,), (0,))
        gram_ref[...] += dot(high, high, along) + dot(high, low, along) + dot(low, high, along)

    half_rows = state // NC
    piece_rows = half_rows // (NX * NY)
    mine_half = pl.ds(pl.multiple_of(c * half_rows, half_rows), half_rows)
    other_half = pl.ds(pl.multiple_of((1 - c) * half_rows, half_rows), half_rows)
    partner = {"rows": row_index(0, 0, 1)}
    pair = pltpu.make_async_remote_copy(
        gram_ref.at[other_half], pair_ref, pair_sem.at[0], pair_sem.at[1], device_id=partner, device_id_type=MESH
    )
    pair.start()

    smalls[3].wait()
    prior = prior_ref[...]
    prior_gram_ref[...] = exact_dot(prior, prior, ((0,), (0,)))
    sort_group(1)
    pair.wait_recv()
    half_ref[...] = gram_ref[mine_half, :] + pair_ref[...]

    def piece(px, py):
        return pl.ds(pl.multiple_of((px * NY + py) * piece_rows, piece_rows), piece_rows)

    plane = [(dx, dy) for dx in range(NX) for dy in range(NY) if (dx, dy) != (0, 0)]
    plane_copies = []
    for n, (dx, dy) in enumerate(plane):
        px, py = (x + dx) % NX, (y + dy) % NY
        copy = pltpu.make_async_remote_copy(
            half_ref.at[piece(px, py)], plane_ref.at[n], plane_sem.at[0, n], plane_sem.at[1, n],
            device_id={"rows": row_index(0, dx, 0), "grp": py}, device_id_type=MESH,
        )
        copy.start()
        plane_copies.append(copy)
    send_group(1, 0, 4)
    sort_group(2)
    for copy in plane_copies:
        copy.wait_recv()
    total = half_ref[piece(x, y), :]
    for n in range(len(plane)):
        total = total + plane_ref[n]
    for t in range(NZ):
        tiles_ref[t] = total[8 * (t // 4) : 8 * (t // 4) + 8, 128 * (t % 4) : 128 * (t % 4) + 128]
    line_copies = []
    for dz in range(1, NZ):
        copy = pltpu.make_async_remote_copy(
            tiles_ref.at[(z + dz) % NZ], line_ref.at[dz], line_sem.at[0, dz], line_sem.at[1, dz],
            device_id={"rows": row_index(dz, 0, 0)}, device_id_type=MESH,
        )
        copy.start()
        line_copies.append(copy)
    send_group(1, 4, 8)
    sort_group(3)
    for copy in line_copies:
        copy.wait_recv()
    done = tiles_ref[z]
    for dz in range(1, NZ):
        done = done + line_ref[dz]
    gather_ref[z] = done
    back_copies = []
    for dz in range(1, NZ):
        copy = pltpu.make_async_remote_copy(
            gather_ref.at[z], gather_ref.at[z], line_back_sem.at[0, dz], line_back_sem.at[1, dz],
            device_id={"rows": row_index(dz, 0, 0)}, device_id_type=MESH,
        )
        copy.start()
        back_copies.append(copy)
    send_group(2, 0, 4)
    sort_group(4)
    for copy in back_copies:
        copy.wait_recv()
    own_piece = pl.ds(
        pl.multiple_of(c * half_rows + (x * NY + y) * piece_rows, piece_rows), piece_rows
    )
    info_ref[own_piece, :] = jnp.concatenate(
        [jnp.concatenate([gather_ref[4 * a + b] for b in range(4)], axis=1) for a in range(2)], axis=0
    )
    plane_back = []
    for n, (dx, dy) in enumerate(plane):
        copy = pltpu.make_async_remote_copy(
            info_ref.at[own_piece], info_ref.at[own_piece], plane_back_sem.at[0, n], plane_back_sem.at[1, n],
            device_id={"rows": row_index(0, dx, 0), "grp": (y + dy) % NY}, device_id_type=MESH,
        )
        copy.start()
        plane_back.append(copy)
    send_group(2, 4, 8)
    sort_group(5)
    for copy in plane_back:
        copy.wait_recv()
    pair_back = pltpu.make_async_remote_copy(
        info_ref.at[mine_half], info_ref.at[mine_half], pair_back_sem.at[0], pair_back_sem.at[1],
        device_id=partner, device_id_type=MESH,
    )
    pair_back.start()
    send_group(3, 0, 4)
    sort_group(6)
    for copies in ([pair], plane_copies, line_copies, back_copies, plane_back):
        for copy in copies:
            copy.wait_send()
    pair_back.wait()
    send_group(3, 4, 8)

    @pl.loop(4, 7)
    def _(g):
        send(g)

    sort_group(7)
    send_group(7)

    gram_ref[...] = prior_gram_ref[...] + info_ref[...] / jnp.float32(total_rows)
    factor_and_invert(gram_ref, factor_ref, inv_ref)
    inv_high_ref[...], inv_low_ref[...] = split(inv_ref[...])

    @pl.loop(0, groups)
    def _(g):
        for j in range(per_group):
            if STEPS[j] == 0:
                @pl.when(jnp.logical_not(is_own(g, j)))
                def _():
                    row_copy(g, j).wait()
            else:
                row_copy(g, j).wait()
        part = pl.ds(pl.multiple_of(g * chunk, chunk), chunk)
        high, low = split(recv_ref[part, :])
        inv_high, inv_low = inv_high_ref[...], inv_low_ref[...]
        cross = ((1,), (1,))
        white = dot(high, inv_high, cross) + dot(high, inv_low, cross) + dot(low, inv_high, cross)
        for j in range(per_group):
            dz, dx, dc = offsets(g, j)
            source = row_index(NZ - dz, NX - dx, NC - dc)
            spot = pl.ds(pl.multiple_of(source * block, block), block)
            out_ref[spot, :] = white[j * block : (j + 1) * block]


def copy_out(white_ref, factor_ref, white_out, factor_out, sem):
    copies = [
        pltpu.make_async_copy(white_ref, white_out, sem.at[0]),
        pltpu.make_async_copy(factor_ref, factor_out, sem.at[1]),
    ]
    for copy in copies:
        copy.start()
    for copy in copies:
        copy.wait()


def shards(observations, sensor_ids, sensor_sigma, buckets, prior_factor):
    rows_dev, state = observations.shape
    total_rows = rows_dev * lax.axis_size(("rows", "grp"))
    vmem = pl.BlockSpec(memory_space=pltpu.VMEM)
    half = state // NC
    piece = half // (NX * NY)
    dma = pltpu.SemaphoreType.DMA
    whitened, factor = pl.pallas_call(
        functools.partial(kernel, total_rows),
        out_shape=(pltpu.VMEM((rows_dev, state), F32), pltpu.VMEM((state, state), F32)),
        in_specs=[pl.BlockSpec(memory_space=pltpu.HBM)] * 5,
        out_specs=(vmem, vmem),
        scratch_shapes=[
            pltpu.VMEM((rows_dev // 128, 128), I32),
            pltpu.VMEM((1, sensor_sigma.shape[0]), F32),
            pltpu.VMEM((rows_dev // 128, 128), I32),
            pltpu.VMEM((state, state), F32),
            pltpu.VMEM((rows_dev, state), F32),
            pltpu.VMEM((rows_dev, state), BF16),
            pltpu.VMEM((rows_dev, state), BF16),
            pltpu.VMEM((rows_dev // (NX * NC), rows_dev), BF16),
            pltpu.VMEM((8, rows_dev), I32),
            pltpu.VMEM((rows_dev, 128), F32),
            pltpu.VMEM((rows_dev, state), F32),
            pltpu.VMEM((rows_dev, state), F32),
            pltpu.VMEM((state, state), F32),
            pltpu.VMEM((half, state), F32),
            pltpu.VMEM((half, state), F32),
            pltpu.VMEM((NX * NY - 1, piece, state), F32),
            pltpu.VMEM((NZ, 8, 128), F32),
            pltpu.VMEM((NZ, 8, 128), F32),
            pltpu.VMEM((NZ, 8, 128), F32),
            pltpu.VMEM((state, state), F32),
            pltpu.VMEM((state, state), F32),
            pltpu.VMEM((state, state), F32),
            pltpu.VMEM((state, state), BF16),
            pltpu.VMEM((state, state), BF16),
            dma((4,)),
            dma((NX * NC,)),
            dma((NZ * NX * NC,)),
            dma((NZ * NX * NC,)),
            dma((2,)),
            dma((2, NX * NY - 1)),
            dma((2, NZ)),
            dma((2, NZ)),
            dma((2, NX * NY - 1)),
            dma((2,)),
        ],
        compiler_params=pltpu.CompilerParams(
            collective_id=0, has_side_effects=True, vmem_limit_bytes=34 << 20
        ),
    )(
        *(
            pltpu.with_memory_space_constraint(array, pltpu.HBM)
            for array in (
                observations,
                sensor_ids.reshape(-1, 128),
                sensor_sigma.reshape(1, -1),
                buckets.reshape(-1, 128),
                prior_factor,
            )
        )
    )
    return pl.pallas_call(
        copy_out,
        out_shape=(
            jax.ShapeDtypeStruct((rows_dev, state), F32),
            jax.ShapeDtypeStruct((state, state), F32),
        ),
        in_specs=[pl.BlockSpec(memory_space=pl.ANY)] * 2,
        out_specs=(pl.BlockSpec(memory_space=pl.ANY),) * 2,
        scratch_shapes=[dma((2,))],
        compiler_params=pltpu.CompilerParams(vmem_limit_bytes=1 << 20),
    )(*(pltpu.with_memory_space_constraint(array, pltpu.VMEM) for array in (whitened, factor)))


def solution(mesh):
    in_specs = (P(("rows", "grp"), None), P(("rows", "grp")), P(), P(("rows", "grp")), P())
    out_specs = (P(("rows", "grp"), None), P())
    return jax.shard_map(shards, mesh=mesh, in_specs=in_specs, out_specs=out_specs, check_vma=False)
```

```python
import functools

import jax
import jax.numpy as jnp
from jax import lax
from jax.experimental import pallas as pl
from jax.experimental.pallas import tpu as pltpu
from jax.sharding import PartitionSpec as P

MESH = pl.DeviceIdType.MESH
F32, BF16, I32 = jnp.float32, jnp.bfloat16, jnp.int32
NZ, NX, NC, NY = 8, 4, 2, 4
STEPS = (4, 1, 7, 3, 5, 2, 6, 0)
PANEL = 128
PACE = 6


def iota(shape, dim):
    return lax.broadcasted_iota(I32, shape, dim)


def split(values):
    high = values.astype(BF16)
    return high, (values - high.astype(F32)).astype(BF16)


def dot(left, right, dims=((1,), (0,))):
    return lax.dot_general(left, right, (dims, ((), ())), preferred_element_type=F32)


def exact_dot(left, right, dims=((1,), (0,))):
    return lax.dot_general(
        left, right, (dims, ((), ())), precision=lax.Precision.HIGHEST, preferred_element_type=F32
    )


def along(piece):
    return jnp.broadcast_to(piece, (8, PANEL))


def root_of(value):
    root = lax.rsqrt(value)
    return root, root * root


def inverse_panel(block):
    tiles = PANEL // 8
    lane, sub = iota((8, PANEL), 1), iota((8, PANEL), 0)
    zero = jnp.float32(0.0)
    rows = [block[8 * q : 8 * q + 8] for q in range(tiles)]
    invs = [jnp.where(lane == sub + 8 * q, jnp.float32(1.0), zero) for q in range(tiles)]
    outs = []
    for p in range(tiles):
        scale = jnp.zeros((8, PANEL), F32)
        for k in (0, 4):
            cols = {
                q: [along(rows[q][:, 8 * p + k + n : 8 * p + k + n + 1]) for n in range(4)] for q in range(p, tiles)
            }
            m = [[along(cols[p][n][k + i : k + i + 1]) for n in range(4)] for i in range(4)]
            a, b, d = m[0][0], m[1][0], m[1][1]
            det = a * d - b * b
            root_a, inv_a = root_of(a)
            root_det, inv_det = root_of(det)
            b02, b03, b12, b13 = m[2][0], m[3][0], m[2][1], m[3][1]
            g02, g12 = (d * b02 - b * b12) * inv_det, (a * b12 - b * b02) * inv_det
            g03, g13 = (d * b03 - b * b13) * inv_det, (a * b13 - b * b03) * inv_det
            s22 = m[2][2] - b02 * g02 - b12 * g12
            s32 = m[3][2] - b03 * g02 - b13 * g12
            s33 = m[3][3] - b03 * g03 - b13 * g13
            low_det = s22 * s33 - s32 * s32
            root_s, inv_s = root_of(s22)
            root_low, inv_low = root_of(low_det)
            f, h = b * inv_a, s32 * inv_s
            for i, root in enumerate((root_a, root_det * (a * root_a), root_s, root_low * (s22 * root_s))):
                scale = jnp.where(sub == k + i, root, scale)

            def eliminate(t0, t1, t2, t3):
                t2 = t2 - g02 * t0 - g12 * t1
                t3 = t3 - g03 * t0 - g13 * t1
                return t0, t1 - f * t0, t2, t3 - h * t2

            weights = (inv_a, a * inv_det, inv_s, s22 * inv_low)
            pivot_rows = eliminate(*(along(rows[p][k + i : k + i + 1]) for i in range(4)))
            pivot_invs = eliminate(*(along(invs[p][k + i : k + i + 1]) for i in range(4)))
            pivot_rows = [value * w for value, w in zip(pivot_rows, weights)]
            pivot_invs = [value * w for value, w in zip(pivot_invs, weights)]
            for q in range(p, tiles):
                x = eliminate(*cols[q])
                if q == p:
                    x = [jnp.where(sub > k + i, x[i], zero) for i in range(4)]
                for held, pivots in ((rows, pivot_rows), (invs, pivot_invs)):
                    held[q] = held[q] - (
                        (x[0] * pivots[0] + x[1] * pivots[1]) + (x[2] * pivots[2] + x[3] * pivots[3])
                    )
        outs.append(invs[p] * scale)
    return jnp.concatenate(outs, axis=0)


def factor_and_invert(matrix_ref, factor_ref, inv_ref):
    state = matrix_ref.shape[0]
    panels = state // PANEL
    factor_ref[...] = jnp.zeros_like(factor_ref)
    down = ((0,), (0,))

    @pl.loop(0, panels)
    def _(k):
        part = pl.ds(pl.multiple_of(k * PANEL, PANEL), PANEL)
        inverse = inverse_panel(matrix_ref[part, part])
        for s in range(panels):

            @pl.when(k == s)
            def _():
                first, last = s * PANEL, (s + 1) * PANEL
                own = slice(first, last)
                wide = exact_dot(inverse, matrix_ref[own, first:])
                keep = iota((PANEL, PANEL), 1) >= iota((PANEL, PANEL), 0)
                factor_ref[own, own] = jnp.where(keep, wide[:, :PANEL], jnp.float32(0.0))
                inv_ref[own, own] = inverse
                if s:
                    inv_ref[own, :first] = exact_dot(inverse, inv_ref[own, :first])
                if s < panels - 1:
                    rest = wide[:, PANEL:]
                    factor_ref[own, last:] = rest
                    inv_ref[own, last:] = jnp.zeros((PANEL, state - last), F32)
                    matrix_ref[last:, last:] = matrix_ref[last:, last:] - exact_dot(rest, rest, down)
                    delta = exact_dot(rest, inv_ref[own, :last], down)
                    if s:
                        inv_ref[last:, :first] = inv_ref[last:, :first] - delta[:, :first]
                    inv_ref[last:, own] = -delta[:, first:]


def kernel(
    total_rows,
    x_hbm, ids_hbm, sigma_hbm, buckets_hbm, prior_hbm,
    out_ref, factor_ref,
    ids_ref, sigma_ref, buckets_ref, prior_ref, x_buf, high_ref, low_ref, pick_ref, target_ref, scale_ref, sorted_ref, recv_ref,
    gram_ref, pair_ref, half_ref, plane_ref, tiles_ref, line_ref, gather_ref, info_ref, inv_ref, prior_gram_ref,
    inv_high_ref, inv_low_ref,
    small_sem, x_sem, send_sem, recv_sem, pair_sem, plane_sem, line_sem, line_back_sem, plane_back_sem, pair_back_sem,
):
    me, y = lax.axis_index("rows"), lax.axis_index("grp")
    z, x, c = me // (NX * NC), (me // NC) % NX, me % NC
    rows_dev, state = x_hbm.shape
    groups, per_group = NX * NC, NZ
    block = rows_dev // (NZ * NX * NC)
    chunk = block * per_group

    def row_index(dz, dx, dc):
        return (((z + dz) % NZ) * NX + (x + dx) % NX) * NC + (c + dc) % NC

    smalls = [
        pltpu.make_async_copy(source, target, small_sem.at[n])
        for n, (source, target) in enumerate(
            ((buckets_hbm, buckets_ref), (ids_hbm, ids_ref), (sigma_hbm, sigma_ref), (prior_hbm, prior_ref))
        )
    ]
    for copy in smalls[:3]:
        copy.start()
    def load(n):
        part = pl.ds(pl.multiple_of(n * 2 * chunk, 2 * chunk), 2 * chunk)
        return pltpu.make_async_copy(x_hbm.at[part], x_buf.at[part], x_sem.at[n])

    for n in range(groups // 2):
        load(n).start()
    smalls[3].start()

    barrier = pltpu.get_barrier_semaphore()
    for dz in range(NZ):
        for dx in range(NX):
            for dc in range(NC):
                if (dz, dx, dc) != (0, 0, 0):
                    pl.semaphore_signal(
                        barrier, inc=1, device_id={"rows": row_index(dz, dx, dc)}, device_id_type=MESH
                    )
    for dx in range(NX):
        for dy in range(1, NY):
            peer = {"rows": row_index(0, dx, 0), "grp": (y + dy) % NY}
            pl.semaphore_signal(barrier, inc=1, device_id=peer, device_id_type=MESH)

    smalls[0].wait()

    n_buckets, n_chunks = NZ * NX * NC, rows_dev // 128
    below = (iota((128, 256), 0) <= iota((128, 256), 1)) | (iota((128, 256), 1) >= 128)
    counter = jnp.where(below, jnp.float32(1.0), jnp.float32(0.0)).astype(BF16)
    bucket_no = iota((n_buckets, 128), 0)
    base = jnp.zeros((n_buckets, 128), F32)
    for q in range(n_chunks):
        match = bucket_no == buckets_ref[q : q + 1, :]
        onehot = jnp.where(match, jnp.float32(1.0), jnp.float32(0.0))
        counts = dot(onehot.astype(BF16), counter)
        rank = counts[:, :128] + base
        base = base + counts[:, 128:]
        spot = jnp.where(match, rank.astype(I32) + (bucket_no * block - 1), 0)
        target_ref[:, 128 * q : 128 * q + 128] = jnp.broadcast_to(
            jnp.sum(spot, axis=0, keepdims=True), (8, 128)
        )

    smalls[1].wait()
    smalls[2].wait()

    weights = jnp.broadcast_to(1.0 / sigma_ref[...], (128, 128)).T
    w_high, w_mid = split(weights)
    w_low = (weights - w_high.astype(F32) - w_mid.astype(F32)).astype(BF16)
    sensor_no = iota((128, 128), 0)
    for q in range(n_chunks):
        onehot = jnp.where(sensor_no == ids_ref[q : q + 1, :], jnp.float32(1.0), jnp.float32(0.0)).T.astype(BF16)
        scale_ref[128 * q : 128 * q + 128, :] = (
            dot(onehot, w_high) + dot(onehot, w_mid) + dot(onehot, w_low)
        )

    @pl.loop(0, groups)
    def _(g):
        @pl.when(g % 2 == 0)
        def _():
            load(g // 2).wait()

        part = pl.ds(pl.multiple_of(g * chunk, chunk), chunk)
        scale = scale_ref[part, :]
        for n in range(state // 128):
            cols = slice(128 * n, 128 * n + 128)
            high, low = split(x_buf[part, cols] * scale)
            high_ref[part, cols] = high
            low_ref[part, cols] = low

    pl.semaphore_wait(barrier, NZ * NX * NC - 1 + NX * (NY - 1))

    def offsets(g, j):
        return STEPS[j], (g // NC + j) % NX, g % NC

    def is_own(g, j):
        dz, dx, dc = offsets(g, j)
        return (dz == 0) & (dx == 0) & (dc == 0)

    def row_copy(g, j):
        return blocks_copy(g, j, 1)

    def blocks_copy(g, j, count):
        spot = pl.ds(pl.multiple_of(g * chunk + j * block, block), count * block)
        return pltpu.make_async_remote_copy(
            sorted_ref.at[spot], recv_ref.at[spot],
            send_sem.at[0], recv_sem.at[g],
            device_id={"rows": row_index(*offsets(g, j))}, device_id_type=MESH,
        )

    def sort(g, start=0, stop=NZ):
        for j in range(start, stop):
            first = row_index(*offsets(g, j)) * block
            for i in range(block // 8):
                hit = target_ref[...] == iota((8, rows_dev), 0) + (first + 8 * i)
                pick_ref[j * block + 8 * i : j * block + 8 * i + 8, :] = jnp.where(
                    hit, jnp.float32(1.0), jnp.float32(0.0)
                ).astype(BF16)
        size = (stop - start) * block
        part = pl.ds(pl.multiple_of(g * chunk + start * block, block), size)
        pick = pick_ref[start * block : stop * block, :]
        sorted_ref[part, :] = dot(pick, high_ref[...]) + dot(pick, low_ref[...])

    def send(g, first=0, last=NZ):
        for j in range(first, last):
            if STEPS[j] == 0:
                own = is_own(g, j)
                spot = pl.ds(pl.multiple_of(g * chunk + j * block, block), block)

                @pl.when(own)
                def _():
                    recv_ref[spot, :] = sorted_ref[spot, :]

                @pl.when(jnp.logical_not(own))
                def _():
                    row_copy(g, j).start()
            else:
                row_copy(g, j).start()

    def sort_group(which, start=0, stop=NZ):
        @pl.loop(which, which + 1)
        def _(g):
            sort(g, start, stop)

    def send_slots(first, last):
        while first < last:
            which, start = first // per_group, first % per_group
            stop = min(per_group, start + last - first)

            @pl.loop(which, which + 1)
            def _(g):
                send(g, start, stop)

            first += stop - start

    def send_next(count):
        send_slots(sent[0], sent[0] + count)
        sent[0] += count

    sent = [0]
    sort_group(0, 0, NZ // 2)
    send_next(NZ // 2)
    sort_group(0, NZ // 2, NZ)
    send_next(NZ // 2)

    gram_ref[...] = jnp.zeros_like(gram_ref)

    @pl.loop(0, groups)
    def _(g):
        part = pl.ds(pl.multiple_of(g * chunk, chunk), chunk)
        high, low = high_ref[part, :], low_ref[part, :]
        along = ((0,), (0,))
        gram_ref[...] += dot(high, high, along) + dot(high, low, along) + dot(low, high, along)

    half_rows = state // NC
    piece_rows = half_rows // (NX * NY)
    mine_half = pl.ds(pl.multiple_of(c * half_rows, half_rows), half_rows)
    other_half = pl.ds(pl.multiple_of((1 - c) * half_rows, half_rows), half_rows)
    partner = {"rows": row_index(0, 0, 1)}
    pair = pltpu.make_async_remote_copy(
        gram_ref.at[other_half], pair_ref, pair_sem.at[0], pair_sem.at[1], device_id=partner, device_id_type=MESH
    )
    pair.start()

    smalls[3].wait()
    prior = prior_ref[...]
    prior_gram_ref[...] = exact_dot(prior, prior, ((0,), (0,)))
    sort_group(1)
    send_next(PACE)
    sort_group(2)
    pair.wait_recv()
    half_ref[...] = gram_ref[mine_half, :] + pair_ref[...]

    def piece(px, py):
        return pl.ds(pl.multiple_of((px * NY + py) * piece_rows, piece_rows), piece_rows)

    others = NX * NY - 1

    def whole(source, target, sems):
        return pltpu.make_async_remote_copy(
            source, target, sems.at[0], sems.at[1], device_id=partner, device_id_type=MESH
        )

    plane = [(dx, dy) for dx in range(NX) for dy in range(NY) if (dx, dy) != (0, 0)]
    for n, (dx, dy) in enumerate(plane):
        px, py = (x + dx) % NX, (y + dy) % NY
        copy = pltpu.make_async_remote_copy(
            half_ref.at[piece(px, py)], plane_ref.at[n], plane_sem.at[0], plane_sem.at[1],
            device_id={"rows": row_index(0, dx, 0), "grp": py}, device_id_type=MESH,
        )
        copy.start()
    send_next(PACE)
    sort_group(3)
    plane_all = whole(half_ref.at[pl.ds(0, others * piece_rows)], plane_ref, plane_sem)
    plane_all.wait_recv()
    total = half_ref[piece(x, y), :]
    for n in range(len(plane)):
        total = total + plane_ref[n]
    for t in range(NZ):
        tiles_ref[t] = total[8 * (t // 4) : 8 * (t // 4) + 8, 128 * (t % 4) : 128 * (t % 4) + 128]
    for dz in range(1, NZ):
        copy = pltpu.make_async_remote_copy(
            tiles_ref.at[(z + dz) % NZ], line_ref.at[dz - 1], line_sem.at[0], line_sem.at[1],
            device_id={"rows": row_index(dz, 0, 0)}, device_id_type=MESH,
        )
        copy.start()
    send_next(PACE)
    sort_group(4)
    line_all = whole(tiles_ref.at[pl.ds(0, NZ - 1)], line_ref, line_sem)
    line_all.wait_recv()
    done = tiles_ref[z]
    for dz in range(1, NZ):
        done = done + line_ref[dz - 1]
    gather_ref[z] = done
    for dz in range(1, NZ):
        copy = pltpu.make_async_remote_copy(
            gather_ref.at[z], gather_ref.at[z], line_back_sem.at[0], line_back_sem.at[1],
            device_id={"rows": row_index(dz, 0, 0)}, device_id_type=MESH,
        )
        copy.start()
    send_next(PACE)
    sort_group(5)
    back_tiles = gather_ref.at[pl.ds(0, NZ - 1)]
    back_all = whole(back_tiles, back_tiles, line_back_sem)
    back_all.wait_recv()
    own_piece = pl.ds(
        pl.multiple_of(c * half_rows + (x * NY + y) * piece_rows, piece_rows), piece_rows
    )
    info_ref[own_piece, :] = jnp.concatenate(
        [jnp.concatenate([gather_ref[4 * a + b] for b in range(4)], axis=1) for a in range(2)], axis=0
    )
    for n, (dx, dy) in enumerate(plane):
        copy = pltpu.make_async_remote_copy(
            info_ref.at[own_piece], info_ref.at[own_piece], plane_back_sem.at[0], plane_back_sem.at[1],
            device_id={"rows": row_index(0, dx, 0), "grp": (y + dy) % NY}, device_id_type=MESH,
        )
        copy.start()
    send_next(PACE)
    sort_group(6)
    back_pieces = info_ref.at[pl.ds(0, others * piece_rows)]
    plane_back_all = whole(back_pieces, back_pieces, plane_back_sem)
    plane_back_all.wait_recv()
    pair_back = pltpu.make_async_remote_copy(
        info_ref.at[mine_half], info_ref.at[mine_half], pair_back_sem.at[0], pair_back_sem.at[1],
        device_id=partner, device_id_type=MESH,
    )
    pair_back.start()
    send_next(PACE)
    sort_group(7)
    for copy in (pair, plane_all, line_all, back_all, plane_back_all):
        copy.wait_send()
    pair_back.wait()
    send_next(-sent[0] % per_group)

    @pl.loop(sent[0] // per_group, groups - 1)
    def _(g):
        send(g)

    send_slots((groups - 1) * per_group, groups * per_group)

    gram_ref[...] = prior_gram_ref[...] + info_ref[...] / jnp.float32(total_rows)
    factor_and_invert(gram_ref, factor_ref, inv_ref)
    inv_high_ref[...], inv_low_ref[...] = split(inv_ref[...])

    @pl.loop(0, groups)
    def _(g):
        own = is_own(g, per_group - 1)

        @pl.when(own)
        def _():
            blocks_copy(g, 0, per_group - 1).wait_recv()

        @pl.when(jnp.logical_not(own))
        def _():
            blocks_copy(g, 0, per_group).wait_recv()

        part = pl.ds(pl.multiple_of(g * chunk, chunk), chunk)
        high, low = split(recv_ref[part, :])
        inv_high, inv_low = inv_high_ref[...], inv_low_ref[...]
        cross = ((1,), (1,))
        white = dot(high, inv_high, cross) + dot(high, inv_low, cross) + dot(low, inv_high, cross)
        for j in range(per_group):
            dz, dx, dc = offsets(g, j)
            source = row_index(NZ - dz, NX - dx, NC - dc)
            spot = pl.ds(pl.multiple_of(source * block, block), block)
            out_ref[spot, :] = white[j * block : (j + 1) * block]

    blocks_copy(0, 0, groups * per_group - 1).wait_send()


def copy_out(white_ref, factor_ref, white_out, factor_out, sem):
    copies = [
        pltpu.make_async_copy(white_ref, white_out, sem.at[0]),
        pltpu.make_async_copy(factor_ref, factor_out, sem.at[1]),
    ]
    for copy in copies:
        copy.start()
    for copy in copies:
        copy.wait()


def shards(observations, sensor_ids, sensor_sigma, buckets, prior_factor):
    rows_dev, state = observations.shape
    total_rows = rows_dev * lax.axis_size(("rows", "grp"))
    vmem = pl.BlockSpec(memory_space=pltpu.VMEM)
    half = state // NC
    piece = half // (NX * NY)
    dma = pltpu.SemaphoreType.DMA
    whitened, factor = pl.pallas_call(
        functools.partial(kernel, total_rows),
        out_shape=(pltpu.VMEM((rows_dev, state), F32), pltpu.VMEM((state, state), F32)),
        in_specs=[pl.BlockSpec(memory_space=pltpu.HBM)] * 5,
        out_specs=(vmem, vmem),
        scratch_shapes=[
            pltpu.VMEM((rows_dev // 128, 128), I32),
            pltpu.VMEM((1, sensor_sigma.shape[0]), F32),
            pltpu.VMEM((rows_dev // 128, 128), I32),
            pltpu.VMEM((state, state), F32),
            pltpu.VMEM((rows_dev, state), F32),
            pltpu.VMEM((rows_dev, state), BF16),
            pltpu.VMEM((rows_dev, state), BF16),
            pltpu.VMEM((rows_dev // (NX * NC), rows_dev), BF16),
            pltpu.VMEM((8, rows_dev), I32),
            pltpu.VMEM((rows_dev, 128), F32),
            pltpu.VMEM((rows_dev, state), F32),
            pltpu.VMEM((rows_dev, state), F32),
            pltpu.VMEM((state, state), F32),
            pltpu.VMEM((half, state), F32),
            pltpu.VMEM((half, state), F32),
            pltpu.VMEM((NX * NY - 1, piece, state), F32),
            pltpu.VMEM((NZ, 8, 128), F32),
            pltpu.VMEM((NZ - 1, 8, 128), F32),
            pltpu.VMEM((NZ, 8, 128), F32),
            pltpu.VMEM((state, state), F32),
            pltpu.VMEM((state, state), F32),
            pltpu.VMEM((state, state), F32),
            pltpu.VMEM((state, state), BF16),
            pltpu.VMEM((state, state), BF16),
            dma((4,)),
            dma((NX * NC // 2,)),
            dma((1,)),
            dma((NX * NC,)),
            dma((2,)),
            dma((2,)),
            dma((2,)),
            dma((2,)),
            dma((2,)),
            dma((2,)),
        ],
        compiler_params=pltpu.CompilerParams(
            collective_id=0, has_side_effects=True, vmem_limit_bytes=34 << 20
        ),
    )(
        *(
            pltpu.with_memory_space_constraint(array, pltpu.HBM)
            for array in (
                observations,
                sensor_ids.reshape(-1, 128),
                sensor_sigma.reshape(1, -1),
                buckets.reshape(-1, 128),
                prior_factor,
            )
        )
    )
    return pl.pallas_call(
        copy_out,
        out_shape=(
            jax.ShapeDtypeStruct((rows_dev, state), F32),
            jax.ShapeDtypeStruct((state, state), F32),
        ),
        in_specs=[pl.BlockSpec(memory_space=pl.ANY)] * 2,
        out_specs=(pl.BlockSpec(memory_space=pl.ANY),) * 2,
        scratch_shapes=[dma((2,))],
        compiler_params=pltpu.CompilerParams(vmem_limit_bytes=1 << 20),
    )(*(pltpu.with_memory_space_constraint(array, pltpu.VMEM) for array in (whitened, factor)))


def solution(mesh):
    in_specs = (P(("rows", "grp"), None), P(("rows", "grp")), P(), P(("rows", "grp")), P())
    out_specs = (P(("rows", "grp"), None), P())
    return jax.shard_map(shards, mesh=mesh, in_specs=in_specs, out_specs=out_specs, check_vma=False)
```

```python
import functools

import jax
import jax.numpy as jnp
from jax import lax
from jax.experimental import pallas as pl
from jax.experimental.pallas import tpu as pltpu
from jax.sharding import PartitionSpec as P

MESH = pl.DeviceIdType.MESH
F32, BF16, I32 = jnp.float32, jnp.bfloat16, jnp.int32
NZ, NX, NC, NY = 8, 4, 2, 4
STEPS = (4, 1, 7, 3, 5, 2, 6, 0)
PANEL = 128
PACE = 6


def iota(shape, dim):
    return lax.broadcasted_iota(I32, shape, dim)


def split(values):
    high = values.astype(BF16)
    return high, (values - high.astype(F32)).astype(BF16)


def dot(left, right, dims=((1,), (0,))):
    return lax.dot_general(left, right, (dims, ((), ())), preferred_element_type=F32)


def exact_dot(left, right, dims=((1,), (0,))):
    return lax.dot_general(
        left, right, (dims, ((), ())), precision=lax.Precision.HIGHEST, preferred_element_type=F32
    )


def along(piece):
    return jnp.broadcast_to(piece, (8, PANEL))


def root_of(value):
    root = lax.rsqrt(value)
    return root, root * root


def inverse_panel(block):
    tiles = PANEL // 8
    lane, sub = iota((8, PANEL), 1), iota((8, PANEL), 0)
    zero = jnp.float32(0.0)
    rows = [block[8 * q : 8 * q + 8] for q in range(tiles)]
    invs = [jnp.where(lane == sub + 8 * q, jnp.float32(1.0), zero) for q in range(tiles)]
    outs = []
    for p in range(tiles):
        scale = jnp.zeros((8, PANEL), F32)
        for k in (0, 4):
            cols = {
                q: [along(rows[q][:, 8 * p + k + n : 8 * p + k + n + 1]) for n in range(4)] for q in range(p, tiles)
            }
            m = [[along(cols[p][n][k + i : k + i + 1]) for n in range(4)] for i in range(4)]
            a, b, d = m[0][0], m[1][0], m[1][1]
            det = a * d - b * b
            root_a, inv_a = root_of(a)
            root_det, inv_det = root_of(det)
            b02, b03, b12, b13 = m[2][0], m[3][0], m[2][1], m[3][1]
            g02, g12 = (d * b02 - b * b12) * inv_det, (a * b12 - b * b02) * inv_det
            g03, g13 = (d * b03 - b * b13) * inv_det, (a * b13 - b * b03) * inv_det
            s22 = m[2][2] - b02 * g02 - b12 * g12
            s32 = m[3][2] - b03 * g02 - b13 * g12
            s33 = m[3][3] - b03 * g03 - b13 * g13
            low_det = s22 * s33 - s32 * s32
            root_s, inv_s = root_of(s22)
            root_low, inv_low = root_of(low_det)
            f, h = b * inv_a, s32 * inv_s
            for i, root in enumerate((root_a, root_det * (a * root_a), root_s, root_low * (s22 * root_s))):
                scale = jnp.where(sub == k + i, root, scale)

            def eliminate(t0, t1, t2, t3):
                t2 = t2 - g02 * t0 - g12 * t1
                t3 = t3 - g03 * t0 - g13 * t1
                return t0, t1 - f * t0, t2, t3 - h * t2

            weights = (inv_a, a * inv_det, inv_s, s22 * inv_low)
            pivot_rows = eliminate(*(along(rows[p][k + i : k + i + 1]) for i in range(4)))
            pivot_invs = eliminate(*(along(invs[p][k + i : k + i + 1]) for i in range(4)))
            pivot_rows = [value * w for value, w in zip(pivot_rows, weights)]
            pivot_invs = [value * w for value, w in zip(pivot_invs, weights)]
            for q in range(p, tiles):
                x = eliminate(*cols[q])
                if q == p:
                    x = [jnp.where(sub > k + i, x[i], zero) for i in range(4)]
                for held, pivots in ((rows, pivot_rows), (invs, pivot_invs)):
                    held[q] = held[q] - (
                        (x[0] * pivots[0] + x[1] * pivots[1]) + (x[2] * pivots[2] + x[3] * pivots[3])
                    )
        outs.append(invs[p] * scale)
    return jnp.concatenate(outs, axis=0)


def factor_and_invert(matrix_ref, factor_ref, inv_ref):
    state = matrix_ref.shape[0]
    panels = state // PANEL
    factor_ref[...] = jnp.zeros_like(factor_ref)
    down = ((0,), (0,))

    @pl.loop(0, panels)
    def _(k):
        part = pl.ds(pl.multiple_of(k * PANEL, PANEL), PANEL)
        inverse = inverse_panel(matrix_ref[part, part])
        for s in range(panels):

            @pl.when(k == s)
            def _():
                first, last = s * PANEL, (s + 1) * PANEL
                own = slice(first, last)
                wide = exact_dot(inverse, matrix_ref[own, first:])
                keep = iota((PANEL, PANEL), 1) >= iota((PANEL, PANEL), 0)
                factor_ref[own, own] = jnp.where(keep, wide[:, :PANEL], jnp.float32(0.0))
                inv_ref[own, own] = inverse
                if s:
                    inv_ref[own, :first] = exact_dot(inverse, inv_ref[own, :first])
                if s < panels - 1:
                    rest = wide[:, PANEL:]
                    factor_ref[own, last:] = rest
                    inv_ref[own, last:] = jnp.zeros((PANEL, state - last), F32)
                    matrix_ref[last:, last:] = matrix_ref[last:, last:] - exact_dot(rest, rest, down)
                    delta = exact_dot(rest, inv_ref[own, :last], down)
                    if s:
                        inv_ref[last:, :first] = inv_ref[last:, :first] - delta[:, :first]
                    inv_ref[last:, own] = -delta[:, first:]


def kernel(
    total_rows,
    x_hbm, ids_hbm, sigma_hbm, buckets_hbm, prior_hbm,
    out_ref, factor_ref,
    ids_ref, sigma_ref, buckets_ref, prior_ref, x_buf, high_ref, low_ref, pick_ref, target_ref, scale_ref, sorted_ref, recv_ref,
    gram_ref, pair_ref, half_ref, plane_ref, tiles_ref, line_ref, gather_ref, info_ref, inv_ref, prior_gram_ref,
    inv_high_ref, inv_low_ref,
    small_sem, x_sem, send_sem, recv_sem, pair_sem, plane_sem, line_sem, line_back_sem, plane_back_sem, pair_back_sem,
):
    me, y = lax.axis_index("rows"), lax.axis_index("grp")
    z, x, c = me // (NX * NC), (me // NC) % NX, me % NC
    rows_dev, state = x_hbm.shape
    groups, per_group = NX * NC, NZ
    block = rows_dev // (NZ * NX * NC)
    chunk = block * per_group

    def row_index(dz, dx, dc):
        return (((z + dz) % NZ) * NX + (x + dx) % NX) * NC + (c + dc) % NC

    barrier = pltpu.get_barrier_semaphore()
    for dz in range(NZ):
        for dx in range(NX):
            for dc in range(NC):
                if (dz, dx, dc) != (0, 0, 0):
                    pl.semaphore_signal(
                        barrier, inc=1, device_id={"rows": row_index(dz, dx, dc)}, device_id_type=MESH
                    )
    for dx in range(NX):
        for dy in range(1, NY):
            peer = {"rows": row_index(0, dx, 0), "grp": (y + dy) % NY}
            pl.semaphore_signal(barrier, inc=1, device_id=peer, device_id_type=MESH)

    smalls = [
        pltpu.make_async_copy(source, target, small_sem.at[n])
        for n, (source, target) in enumerate(
            ((buckets_hbm, buckets_ref), (ids_hbm, ids_ref), (sigma_hbm, sigma_ref), (prior_hbm, prior_ref))
        )
    ]
    for copy in smalls[:3]:
        copy.start()
    def load(n):
        part = pl.ds(pl.multiple_of(n * 2 * chunk, 2 * chunk), 2 * chunk)
        return pltpu.make_async_copy(x_hbm.at[part], x_buf.at[part], x_sem.at[n])

    for n in range(groups // 2):
        load(n).start()
    smalls[3].start()

    smalls[0].wait()

    n_buckets, n_chunks = NZ * NX * NC, rows_dev // 128
    below = (iota((128, 256), 0) <= iota((128, 256), 1)) | (iota((128, 256), 1) >= 128)
    counter = jnp.where(below, jnp.float32(1.0), jnp.float32(0.0)).astype(BF16)
    bucket_no = iota((n_buckets, 128), 0)
    base = jnp.zeros((n_buckets, 128), F32)
    for q in range(n_chunks):
        match = bucket_no == buckets_ref[q : q + 1, :]
        onehot = jnp.where(match, jnp.float32(1.0), jnp.float32(0.0))
        counts = dot(onehot.astype(BF16), counter)
        rank = counts[:, :128] + base
        base = base + counts[:, 128:]
        spot = jnp.where(match, rank.astype(I32) + (bucket_no * block - 1), 0)
        target_ref[:, 128 * q : 128 * q + 128] = jnp.broadcast_to(
            jnp.sum(spot, axis=0, keepdims=True), (8, 128)
        )

    smalls[1].wait()
    smalls[2].wait()

    weights = jnp.broadcast_to(1.0 / sigma_ref[...], (128, 128)).T
    w_high, w_mid = split(weights)
    w_low = (weights - w_high.astype(F32) - w_mid.astype(F32)).astype(BF16)
    sensor_no = iota((128, 128), 0)
    for q in range(n_chunks):
        onehot = jnp.where(sensor_no == ids_ref[q : q + 1, :], jnp.float32(1.0), jnp.float32(0.0)).T.astype(BF16)
        scale_ref[128 * q : 128 * q + 128, :] = (
            dot(onehot, w_high) + dot(onehot, w_mid) + dot(onehot, w_low)
        )

    @pl.loop(0, groups)
    def _(g):
        @pl.when(g % 2 == 0)
        def _():
            load(g // 2).wait()

        part = pl.ds(pl.multiple_of(g * chunk, chunk), chunk)
        scale = scale_ref[part, :]
        for n in range(state // 128):
            cols = slice(128 * n, 128 * n + 128)
            high, low = split(x_buf[part, cols] * scale)
            high_ref[part, cols] = high
            low_ref[part, cols] = low

    def offsets(g, j):
        return STEPS[j], (g // NC + j) % NX, g % NC

    def is_own(g, j):
        dz, dx, dc = offsets(g, j)
        return (dz == 0) & (dx == 0) & (dc == 0)

    def row_copy(g, j):
        return blocks_copy(g, j, 1)

    def blocks_copy(g, j, count):
        spot = pl.ds(pl.multiple_of(g * chunk + j * block, block), count * block)
        return pltpu.make_async_remote_copy(
            sorted_ref.at[spot], recv_ref.at[spot],
            send_sem.at[0], recv_sem.at[g],
            device_id={"rows": row_index(*offsets(g, j))}, device_id_type=MESH,
        )

    def sort(g, start=0, stop=NZ):
        for j in range(start, stop):
            first = row_index(*offsets(g, j)) * block
            for i in range(block // 8):
                hit = target_ref[...] == iota((8, rows_dev), 0) + (first + 8 * i)
                pick_ref[j * block + 8 * i : j * block + 8 * i + 8, :] = jnp.where(
                    hit, jnp.float32(1.0), jnp.float32(0.0)
                ).astype(BF16)
        size = (stop - start) * block
        part = pl.ds(pl.multiple_of(g * chunk + start * block, block), size)
        pick = pick_ref[start * block : stop * block, :]
        sorted_ref[part, :] = dot(pick, high_ref[...]) + dot(pick, low_ref[...])

    def send(g, first=0, last=NZ):
        for j in range(first, last):
            if STEPS[j] == 0:
                own = is_own(g, j)
                spot = pl.ds(pl.multiple_of(g * chunk + j * block, block), block)

                @pl.when(own)
                def _():
                    recv_ref[spot, :] = sorted_ref[spot, :]

                @pl.when(jnp.logical_not(own))
                def _():
                    row_copy(g, j).start()
            else:
                row_copy(g, j).start()

    def sort_group(which, start=0, stop=NZ):
        @pl.loop(which, which + 1)
        def _(g):
            sort(g, start, stop)

    def send_slots(first, last):
        while first < last:
            which, start = first // per_group, first % per_group
            stop = min(per_group, start + last - first)

            @pl.loop(which, which + 1)
            def _(g):
                send(g, start, stop)

            first += stop - start

    def send_next(count):
        send_slots(sent[0], sent[0] + count)
        sent[0] += count

    sent = [0]
    sort_group(0)
    pl.semaphore_wait(barrier, NZ * NX * NC - 1 + NX * (NY - 1))
    send_next(per_group)

    gram_ref[...] = jnp.zeros_like(gram_ref)

    @pl.loop(0, groups)
    def _(g):
        part = pl.ds(pl.multiple_of(g * chunk, chunk), chunk)
        high, low = high_ref[part, :], low_ref[part, :]
        along = ((0,), (0,))
        gram_ref[...] += dot(high, high, along) + dot(high, low, along) + dot(low, high, along)

    half_rows = state // NC
    piece_rows = half_rows // (NX * NY)
    mine_half = pl.ds(pl.multiple_of(c * half_rows, half_rows), half_rows)
    other_half = pl.ds(pl.multiple_of((1 - c) * half_rows, half_rows), half_rows)
    partner = {"rows": row_index(0, 0, 1)}
    pair = pltpu.make_async_remote_copy(
        gram_ref.at[other_half], pair_ref, pair_sem.at[0], pair_sem.at[1], device_id=partner, device_id_type=MESH
    )
    pair.start()

    smalls[3].wait()
    prior = prior_ref[...]
    prior_gram_ref[...] = exact_dot(prior, prior, ((0,), (0,)))
    sort_group(1)
    send_next(PACE)
    sort_group(2)
    pair.wait_recv()
    half_ref[...] = gram_ref[mine_half, :] + pair_ref[...]

    def piece(px, py):
        return pl.ds(pl.multiple_of((px * NY + py) * piece_rows, piece_rows), piece_rows)

    others = NX * NY - 1

    def whole(source, target, sems):
        return pltpu.make_async_remote_copy(
            source, target, sems.at[0], sems.at[1], device_id=partner, device_id_type=MESH
        )

    plane = [(dx, dy) for dx in range(NX) for dy in range(NY) if (dx, dy) != (0, 0)]
    for n, (dx, dy) in enumerate(plane):
        px, py = (x + dx) % NX, (y + dy) % NY
        copy = pltpu.make_async_remote_copy(
            half_ref.at[piece(px, py)], plane_ref.at[n], plane_sem.at[0], plane_sem.at[1],
            device_id={"rows": row_index(0, dx, 0), "grp": py}, device_id_type=MESH,
        )
        copy.start()
    send_next(PACE)
    sort_group(3)
    plane_all = whole(half_ref.at[pl.ds(0, others * piece_rows)], plane_ref, plane_sem)
    plane_all.wait_recv()
    total = half_ref[piece(x, y), :]
    for n in range(len(plane)):
        total = total + plane_ref[n]
    for t in range(NZ):
        tiles_ref[t] = total[8 * (t // 4) : 8 * (t // 4) + 8, 128 * (t % 4) : 128 * (t % 4) + 128]
    for dz in range(1, NZ):
        copy = pltpu.make_async_remote_copy(
            tiles_ref.at[(z + dz) % NZ], line_ref.at[dz - 1], line_sem.at[0], line_sem.at[1],
            device_id={"rows": row_index(dz, 0, 0)}, device_id_type=MESH,
        )
        copy.start()
    send_next(PACE)
    sort_group(4)
    line_all = whole(tiles_ref.at[pl.ds(0, NZ - 1)], line_ref, line_sem)
    line_all.wait_recv()
    done = tiles_ref[z]
    for dz in range(1, NZ):
        done = done + line_ref[dz - 1]
    gather_ref[z] = done
    for dz in range(1, NZ):
        copy = pltpu.make_async_remote_copy(
            gather_ref.at[z], gather_ref.at[z], line_back_sem.at[0], line_back_sem.at[1],
            device_id={"rows": row_index(dz, 0, 0)}, device_id_type=MESH,
        )
        copy.start()
    send_next(PACE)
    sort_group(5)
    back_tiles = gather_ref.at[pl.ds(0, NZ - 1)]
    back_all = whole(back_tiles, back_tiles, line_back_sem)
    back_all.wait_recv()
    own_piece = pl.ds(
        pl.multiple_of(c * half_rows + (x * NY + y) * piece_rows, piece_rows), piece_rows
    )
    info_ref[own_piece, :] = jnp.concatenate(
        [jnp.concatenate([gather_ref[4 * a + b] for b in range(4)], axis=1) for a in range(2)], axis=0
    )
    for n, (dx, dy) in enumerate(plane):
        copy = pltpu.make_async_remote_copy(
            info_ref.at[own_piece], info_ref.at[own_piece], plane_back_sem.at[0], plane_back_sem.at[1],
            device_id={"rows": row_index(0, dx, 0), "grp": (y + dy) % NY}, device_id_type=MESH,
        )
        copy.start()
    send_next(PACE)
    sort_group(6)
    back_pieces = info_ref.at[pl.ds(0, others * piece_rows)]
    plane_back_all = whole(back_pieces, back_pieces, plane_back_sem)
    plane_back_all.wait_recv()
    pair_back = pltpu.make_async_remote_copy(
        info_ref.at[mine_half], info_ref.at[mine_half], pair_back_sem.at[0], pair_back_sem.at[1],
        device_id=partner, device_id_type=MESH,
    )
    pair_back.start()
    send_next(PACE)
    sort_group(7)
    pair.wait_send()
    pair_back.wait_recv()
    send_next(-sent[0] % per_group)

    @pl.loop(sent[0] // per_group, groups - 1)
    def _(g):
        send(g)

    send_slots((groups - 1) * per_group, groups * per_group)

    gram_ref[...] = prior_gram_ref[...] + info_ref[...] / jnp.float32(total_rows)
    factor_and_invert(gram_ref, factor_ref, inv_ref)
    inv_high_ref[...], inv_low_ref[...] = split(inv_ref[...])

    @pl.loop(0, groups)
    def _(g):
        own = is_own(g, per_group - 1)

        @pl.when(own)
        def _():
            blocks_copy(g, 0, per_group - 1).wait_recv()

        @pl.when(jnp.logical_not(own))
        def _():
            blocks_copy(g, 0, per_group).wait_recv()

        part = pl.ds(pl.multiple_of(g * chunk, chunk), chunk)
        high, low = split(recv_ref[part, :])
        inv_high, inv_low = inv_high_ref[...], inv_low_ref[...]
        cross = ((1,), (1,))
        white = dot(high, inv_high, cross) + dot(high, inv_low, cross) + dot(low, inv_high, cross)
        for j in range(per_group):
            dz, dx, dc = offsets(g, j)
            source = row_index(NZ - dz, NX - dx, NC - dc)
            spot = pl.ds(pl.multiple_of(source * block, block), block)
            out_ref[spot, :] = white[j * block : (j + 1) * block]

    blocks_copy(0, 0, groups * per_group - 1).wait_send()
    for copy in (plane_all, line_all, back_all, plane_back_all, pair_back):
        copy.wait_send()


def copy_out(white_ref, factor_ref, white_out, factor_out, sem):
    copies = [
        pltpu.make_async_copy(white_ref, white_out, sem.at[0]),
        pltpu.make_async_copy(factor_ref, factor_out, sem.at[1]),
    ]
    for copy in copies:
        copy.start()
    for copy in copies:
        copy.wait()


def shards(observations, sensor_ids, sensor_sigma, buckets, prior_factor):
    rows_dev, state = observations.shape
    total_rows = rows_dev * lax.axis_size(("rows", "grp"))
    vmem = pl.BlockSpec(memory_space=pltpu.VMEM)
    half = state // NC
    piece = half // (NX * NY)
    dma = pltpu.SemaphoreType.DMA
    whitened, factor = pl.pallas_call(
        functools.partial(kernel, total_rows),
        out_shape=(pltpu.VMEM((rows_dev, state), F32), pltpu.VMEM((state, state), F32)),
        in_specs=[pl.BlockSpec(memory_space=pltpu.HBM)] * 5,
        out_specs=(vmem, vmem),
        scratch_shapes=[
            pltpu.VMEM((rows_dev // 128, 128), I32),
            pltpu.VMEM((1, sensor_sigma.shape[0]), F32),
            pltpu.VMEM((rows_dev // 128, 128), I32),
            pltpu.VMEM((state, state), F32),
            pltpu.VMEM((rows_dev, state), F32),
            pltpu.VMEM((rows_dev, state), BF16),
            pltpu.VMEM((rows_dev, state), BF16),
            pltpu.VMEM((rows_dev // (NX * NC), rows_dev), BF16),
            pltpu.VMEM((8, rows_dev), I32),
            pltpu.VMEM((rows_dev, 128), F32),
            pltpu.VMEM((rows_dev, state), F32),
            pltpu.VMEM((rows_dev, state), F32),
            pltpu.VMEM((state, state), F32),
            pltpu.VMEM((half, state), F32),
            pltpu.VMEM((half, state), F32),
            pltpu.VMEM((NX * NY - 1, piece, state), F32),
            pltpu.VMEM((NZ, 8, 128), F32),
            pltpu.VMEM((NZ - 1, 8, 128), F32),
            pltpu.VMEM((NZ, 8, 128), F32),
            pltpu.VMEM((state, state), F32),
            pltpu.VMEM((state, state), F32),
            pltpu.VMEM((state, state), F32),
            pltpu.VMEM((state, state), BF16),
            pltpu.VMEM((state, state), BF16),
            dma((4,)),
            dma((NX * NC // 2,)),
            dma((1,)),
            dma((NX * NC,)),
            dma((2,)),
            dma((2,)),
            dma((2,)),
            dma((2,)),
            dma((2,)),
            dma((2,)),
        ],
        compiler_params=pltpu.CompilerParams(
            collective_id=0, has_side_effects=True, vmem_limit_bytes=34 << 20
        ),
    )(
        *(
            pltpu.with_memory_space_constraint(array, pltpu.HBM)
            for array in (
                observations,
                sensor_ids.reshape(-1, 128),
                sensor_sigma.reshape(1, -1),
                buckets.reshape(-1, 128),
                prior_factor,
            )
        )
    )
    return pl.pallas_call(
        copy_out,
        out_shape=(
            jax.ShapeDtypeStruct((rows_dev, state), F32),
            jax.ShapeDtypeStruct((state, state), F32),
        ),
        in_specs=[pl.BlockSpec(memory_space=pl.ANY)] * 2,
        out_specs=(pl.BlockSpec(memory_space=pl.ANY),) * 2,
        scratch_shapes=[dma((2,))],
        compiler_params=pltpu.CompilerParams(vmem_limit_bytes=1 << 20),
    )(*(pltpu.with_memory_space_constraint(array, pltpu.VMEM) for array in (whitened, factor)))


def solution(mesh):
    in_specs = (P(("rows", "grp"), None), P(("rows", "grp")), P(), P(("rows", "grp")), P())
    out_specs = (P(("rows", "grp"), None), P())
    return jax.shard_map(shards, mesh=mesh, in_specs=in_specs, out_specs=out_specs, check_vma=False)
```

```python
import functools

import jax
import jax.numpy as jnp
from jax import lax
from jax.experimental import pallas as pl
from jax.experimental.pallas import tpu as pltpu
from jax.sharding import PartitionSpec as P

MESH = pl.DeviceIdType.MESH
F32, BF16, I32 = jnp.float32, jnp.bfloat16, jnp.int32
NZ, NX, NC, NY = 8, 4, 2, 4
STEPS = (4, 1, 7, 3, 5, 2, 6, 0)
PANEL = 128
PACE = 7


def iota(shape, dim):
    return lax.broadcasted_iota(I32, shape, dim)


def split(values):
    high = values.astype(BF16)
    return high, (values - high.astype(F32)).astype(BF16)


def dot(left, right, dims=((1,), (0,))):
    return lax.dot_general(left, right, (dims, ((), ())), preferred_element_type=F32)


def exact_dot(left, right, dims=((1,), (0,))):
    return lax.dot_general(
        left, right, (dims, ((), ())), precision=lax.Precision.HIGHEST, preferred_element_type=F32
    )


def along(piece):
    return jnp.broadcast_to(piece, (8, PANEL))


def root_of(value):
    root = lax.rsqrt(value)
    return root, root * root


def inverse_panel(block):
    tiles = PANEL // 8
    lane, sub = iota((8, PANEL), 1), iota((8, PANEL), 0)
    zero = jnp.float32(0.0)
    rows = [block[8 * q : 8 * q + 8] for q in range(tiles)]
    invs = [jnp.where(lane == sub + 8 * q, jnp.float32(1.0), zero) for q in range(tiles)]
    outs = []
    for p in range(tiles):
        scale = jnp.zeros((8, PANEL), F32)
        for k in (0, 4):
            cols = {
                q: [along(rows[q][:, 8 * p + k + n : 8 * p + k + n + 1]) for n in range(4)] for q in range(p, tiles)
            }
            m = [[along(cols[p][n][k + i : k + i + 1]) for n in range(4)] for i in range(4)]
            a, b, d = m[0][0], m[1][0], m[1][1]
            det = a * d - b * b
            root_a, inv_a = root_of(a)
            root_det, inv_det = root_of(det)
            b02, b03, b12, b13 = m[2][0], m[3][0], m[2][1], m[3][1]
            g02, g12 = (d * b02 - b * b12) * inv_det, (a * b12 - b * b02) * inv_det
            g03, g13 = (d * b03 - b * b13) * inv_det, (a * b13 - b * b03) * inv_det
            s22 = m[2][2] - b02 * g02 - b12 * g12
            s32 = m[3][2] - b03 * g02 - b13 * g12
            s33 = m[3][3] - b03 * g03 - b13 * g13
            low_det = s22 * s33 - s32 * s32
            root_s, inv_s = root_of(s22)
            root_low, inv_low = root_of(low_det)
            f, h = b * inv_a, s32 * inv_s
            for i, root in enumerate((root_a, root_det * (a * root_a), root_s, root_low * (s22 * root_s))):
                scale = jnp.where(sub == k + i, root, scale)

            def eliminate(t0, t1, t2, t3):
                t2 = t2 - g02 * t0 - g12 * t1
                t3 = t3 - g03 * t0 - g13 * t1
                return t0, t1 - f * t0, t2, t3 - h * t2

            weights = (inv_a, a * inv_det, inv_s, s22 * inv_low)
            pivot_rows = eliminate(*(along(rows[p][k + i : k + i + 1]) for i in range(4)))
            pivot_invs = eliminate(*(along(invs[p][k + i : k + i + 1]) for i in range(4)))
            pivot_rows = [value * w for value, w in zip(pivot_rows, weights)]
            pivot_invs = [value * w for value, w in zip(pivot_invs, weights)]
            for q in range(p, tiles):
                x = eliminate(*cols[q])
                if q == p:
                    x = [jnp.where(sub > k + i, x[i], zero) for i in range(4)]
                for held, pivots in ((rows, pivot_rows), (invs, pivot_invs)):
                    held[q] = held[q] - (
                        (x[0] * pivots[0] + x[1] * pivots[1]) + (x[2] * pivots[2] + x[3] * pivots[3])
                    )
        outs.append(invs[p] * scale)
    return jnp.concatenate(outs, axis=0)


def factor_and_invert(matrix_ref, factor_ref, inv_ref):
    state = matrix_ref.shape[0]
    panels = state // PANEL
    factor_ref[...] = jnp.zeros_like(factor_ref)
    down = ((0,), (0,))

    @pl.loop(0, panels)
    def _(k):
        part = pl.ds(pl.multiple_of(k * PANEL, PANEL), PANEL)
        inverse = inverse_panel(matrix_ref[part, part])
        for s in range(panels):

            @pl.when(k == s)
            def _():
                first, last = s * PANEL, (s + 1) * PANEL
                own = slice(first, last)
                wide = exact_dot(inverse, matrix_ref[own, first:])
                keep = iota((PANEL, PANEL), 1) >= iota((PANEL, PANEL), 0)
                factor_ref[own, own] = jnp.where(keep, wide[:, :PANEL], jnp.float32(0.0))
                inv_ref[own, own] = inverse
                if s:
                    inv_ref[own, :first] = exact_dot(inverse, inv_ref[own, :first])
                if s < panels - 1:
                    rest = wide[:, PANEL:]
                    factor_ref[own, last:] = rest
                    inv_ref[own, last:] = jnp.zeros((PANEL, state - last), F32)
                    matrix_ref[last:, last:] = matrix_ref[last:, last:] - exact_dot(rest, rest, down)
                    delta = exact_dot(rest, inv_ref[own, :last], down)
                    if s:
                        inv_ref[last:, :first] = inv_ref[last:, :first] - delta[:, :first]
                    inv_ref[last:, own] = -delta[:, first:]


def kernel(
    total_rows,
    x_hbm, ids_hbm, sigma_hbm, buckets_hbm, prior_hbm,
    out_ref, factor_ref,
    ids_ref, sigma_ref, buckets_ref, prior_ref, x_buf, high_ref, low_ref, pick_ref, target_ref, scale_ref, sorted_ref, recv_ref,
    gram_ref, pair_ref, half_ref, plane_ref, tiles_ref, line_ref, gather_ref, info_ref, inv_ref, prior_gram_ref,
    inv_high_ref, inv_low_ref,
    small_sem, x_sem, send_sem, recv_sem, pair_sem, plane_sem, line_sem, line_back_sem, plane_back_sem, pair_back_sem,
):
    me, y = lax.axis_index("rows"), lax.axis_index("grp")
    z, x, c = me // (NX * NC), (me // NC) % NX, me % NC
    rows_dev, state = x_hbm.shape
    groups, per_group = NX * NC, NZ
    block = rows_dev // (NZ * NX * NC)
    chunk = block * per_group

    def row_index(dz, dx, dc):
        return (((z + dz) % NZ) * NX + (x + dx) % NX) * NC + (c + dc) % NC

    barrier = pltpu.get_barrier_semaphore()
    for dz in range(NZ):
        for dx in range(NX):
            for dc in range(NC):
                if (dz, dx, dc) != (0, 0, 0):
                    pl.semaphore_signal(
                        barrier, inc=1, device_id={"rows": row_index(dz, dx, dc)}, device_id_type=MESH
                    )
    for dx in range(NX):
        for dy in range(1, NY):
            peer = {"rows": row_index(0, dx, 0), "grp": (y + dy) % NY}
            pl.semaphore_signal(barrier, inc=1, device_id=peer, device_id_type=MESH)

    smalls = [
        pltpu.make_async_copy(source, target, small_sem.at[n])
        for n, (source, target) in enumerate(
            ((buckets_hbm, buckets_ref), (ids_hbm, ids_ref), (sigma_hbm, sigma_ref), (prior_hbm, prior_ref))
        )
    ]
    for copy in smalls[:3]:
        copy.start()
    def load(n):
        part = pl.ds(pl.multiple_of(n * 2 * chunk, 2 * chunk), 2 * chunk)
        return pltpu.make_async_copy(x_hbm.at[part], x_buf.at[part], x_sem.at[n])

    for n in range(groups // 2):
        load(n).start()
    smalls[3].start()

    smalls[0].wait()

    n_buckets, n_chunks = NZ * NX * NC, rows_dev // 128
    below = (iota((128, 256), 0) <= iota((128, 256), 1)) | (iota((128, 256), 1) >= 128)
    counter = jnp.where(below, jnp.float32(1.0), jnp.float32(0.0)).astype(BF16)
    bucket_no = iota((n_buckets, 128), 0)
    base = jnp.zeros((n_buckets, 128), F32)
    for q in range(n_chunks):
        match = bucket_no == buckets_ref[q : q + 1, :]
        onehot = jnp.where(match, jnp.float32(1.0), jnp.float32(0.0))
        counts = dot(onehot.astype(BF16), counter)
        rank = counts[:, :128] + base
        base = base + counts[:, 128:]
        spot = jnp.where(match, rank.astype(I32) + (bucket_no * block - 1), 0)
        target_ref[:, 128 * q : 128 * q + 128] = jnp.broadcast_to(
            jnp.sum(spot, axis=0, keepdims=True), (8, 128)
        )

    smalls[1].wait()
    smalls[2].wait()

    weights = jnp.broadcast_to(1.0 / sigma_ref[...], (128, 128)).T
    w_high, w_mid = split(weights)
    w_low = (weights - w_high.astype(F32) - w_mid.astype(F32)).astype(BF16)
    sensor_no = iota((128, 128), 0)
    for q in range(n_chunks):
        onehot = jnp.where(sensor_no == ids_ref[q : q + 1, :], jnp.float32(1.0), jnp.float32(0.0)).T.astype(BF16)
        scale_ref[128 * q : 128 * q + 128, :] = (
            dot(onehot, w_high) + dot(onehot, w_mid) + dot(onehot, w_low)
        )

    @pl.loop(0, groups)
    def _(g):
        @pl.when(g % 2 == 0)
        def _():
            load(g // 2).wait()

        part = pl.ds(pl.multiple_of(g * chunk, chunk), chunk)
        scale = scale_ref[part, :]
        for n in range(state // 128):
            cols = slice(128 * n, 128 * n + 128)
            high, low = split(x_buf[part, cols] * scale)
            high_ref[part, cols] = high
            low_ref[part, cols] = low

    def offsets(g, j):
        return STEPS[j], (g // NC + j) % NX, g % NC

    def is_own(g, j):
        dz, dx, dc = offsets(g, j)
        return (dz == 0) & (dx == 0) & (dc == 0)

    def row_copy(g, j):
        return blocks_copy(g, j, 1)

    def blocks_copy(g, j, count):
        spot = pl.ds(pl.multiple_of(g * chunk + j * block, block), count * block)
        return pltpu.make_async_remote_copy(
            sorted_ref.at[spot], recv_ref.at[spot],
            send_sem.at[0], recv_sem.at[g],
            device_id={"rows": row_index(*offsets(g, j))}, device_id_type=MESH,
        )

    def sort(g, start=0, stop=NZ):
        for j in range(start, stop):
            first = row_index(*offsets(g, j)) * block
            for i in range(block // 8):
                hit = target_ref[...] == iota((8, rows_dev), 0) + (first + 8 * i)
                pick_ref[j * block + 8 * i : j * block + 8 * i + 8, :] = jnp.where(
                    hit, jnp.float32(1.0), jnp.float32(0.0)
                ).astype(BF16)
        size = (stop - start) * block
        part = pl.ds(pl.multiple_of(g * chunk + start * block, block), size)
        pick = pick_ref[start * block : stop * block, :]
        sorted_ref[part, :] = dot(pick, high_ref[...]) + dot(pick, low_ref[...])

    def send(g, first=0, last=NZ):
        for j in range(first, last):
            if STEPS[j] == 0:
                own = is_own(g, j)
                spot = pl.ds(pl.multiple_of(g * chunk + j * block, block), block)

                @pl.when(own)
                def _():
                    recv_ref[spot, :] = sorted_ref[spot, :]

                @pl.when(jnp.logical_not(own))
                def _():
                    row_copy(g, j).start()
            else:
                row_copy(g, j).start()

    def sort_group(which, start=0, stop=NZ):
        @pl.loop(which, which + 1)
        def _(g):
            sort(g, start, stop)

    def send_slots(first, last):
        while first < last:
            which, start = first // per_group, first % per_group
            stop = min(per_group, start + last - first)

            @pl.loop(which, which + 1)
            def _(g):
                send(g, start, stop)

            first += stop - start

    def send_next(count):
        send_slots(sent[0], sent[0] + count)
        sent[0] += count

    sent = [0]
    sort_group(0, 0, per_group // 2)
    pl.semaphore_wait(barrier, NZ * NX * NC - 1 + NX * (NY - 1))
    send_next(per_group // 2)
    sort_group(0, per_group // 2, per_group)
    send_next(2)

    gram_ref[...] = jnp.zeros_like(gram_ref)

    @pl.loop(0, groups // 2)
    def _(g):
        part = pl.ds(pl.multiple_of(g * 2 * chunk, 2 * chunk), 2 * chunk)
        high, low = high_ref[part, :], low_ref[part, :]
        along = ((0,), (0,))
        gram_ref[...] += dot(high, high, along) + dot(high, low, along) + dot(low, high, along)

    half_rows = state // NC
    piece_rows = half_rows // (NX * NY)
    mine_half = pl.ds(pl.multiple_of(c * half_rows, half_rows), half_rows)
    other_half = pl.ds(pl.multiple_of((1 - c) * half_rows, half_rows), half_rows)
    partner = {"rows": row_index(0, 0, 1)}
    pair = pltpu.make_async_remote_copy(
        gram_ref.at[other_half], pair_ref, pair_sem.at[0], pair_sem.at[1], device_id=partner, device_id_type=MESH
    )
    pair.start()
    send_next(per_group // 2 - 2)

    smalls[3].wait()
    prior = prior_ref[...]
    prior_gram_ref[...] = exact_dot(prior, prior, ((0,), (0,)))
    sort_group(1)
    send_next(PACE)
    sort_group(2)
    pair.wait_recv()
    half_ref[...] = gram_ref[mine_half, :] + pair_ref[...]

    def piece(px, py):
        return pl.ds(pl.multiple_of((px * NY + py) * piece_rows, piece_rows), piece_rows)

    others = NX * NY - 1

    def whole(source, target, sems):
        return pltpu.make_async_remote_copy(
            source, target, sems.at[0], sems.at[1], device_id=partner, device_id_type=MESH
        )

    plane = [(dx, dy) for dx in range(NX) for dy in range(NY) if (dx, dy) != (0, 0)]
    for n, (dx, dy) in enumerate(plane):
        px, py = (x + dx) % NX, (y + dy) % NY
        copy = pltpu.make_async_remote_copy(
            half_ref.at[piece(px, py)], plane_ref.at[n], plane_sem.at[0], plane_sem.at[1],
            device_id={"rows": row_index(0, dx, 0), "grp": py}, device_id_type=MESH,
        )
        copy.start()
    send_next(PACE)
    sort_group(3)
    plane_all = whole(half_ref.at[pl.ds(0, others * piece_rows)], plane_ref, plane_sem)
    plane_all.wait_recv()
    total = half_ref[piece(x, y), :]
    for n in range(len(plane)):
        total = total + plane_ref[n]
    for t in range(NZ):
        tiles_ref[t] = total[8 * (t // 4) : 8 * (t // 4) + 8, 128 * (t % 4) : 128 * (t % 4) + 128]
    for dz in range(1, NZ):
        copy = pltpu.make_async_remote_copy(
            tiles_ref.at[(z + dz) % NZ], line_ref.at[dz - 1], line_sem.at[0], line_sem.at[1],
            device_id={"rows": row_index(dz, 0, 0)}, device_id_type=MESH,
        )
        copy.start()
    send_next(PACE)
    sort_group(4)
    line_all = whole(tiles_ref.at[pl.ds(0, NZ - 1)], line_ref, line_sem)
    line_all.wait_recv()
    done = tiles_ref[z]
    for dz in range(1, NZ):
        done = done + line_ref[dz - 1]
    gather_ref[z] = done
    for dz in range(1, NZ):
        copy = pltpu.make_async_remote_copy(
            gather_ref.at[z], gather_ref.at[z], line_back_sem.at[0], line_back_sem.at[1],
            device_id={"rows": row_index(dz, 0, 0)}, device_id_type=MESH,
        )
        copy.start()
    send_next(PACE)
    sort_group(5)
    back_tiles = gather_ref.at[pl.ds(0, NZ - 1)]
    back_all = whole(back_tiles, back_tiles, line_back_sem)
    back_all.wait_recv()
    own_piece = pl.ds(
        pl.multiple_of(c * half_rows + (x * NY + y) * piece_rows, piece_rows), piece_rows
    )
    info_ref[own_piece, :] = jnp.concatenate(
        [jnp.concatenate([gather_ref[4 * a + b] for b in range(4)], axis=1) for a in range(2)], axis=0
    )
    for n, (dx, dy) in enumerate(plane):
        copy = pltpu.make_async_remote_copy(
            info_ref.at[own_piece], info_ref.at[own_piece], plane_back_sem.at[0], plane_back_sem.at[1],
            device_id={"rows": row_index(0, dx, 0), "grp": (y + dy) % NY}, device_id_type=MESH,
        )
        copy.start()
    send_next(PACE)
    sort_group(6)
    back_pieces = info_ref.at[pl.ds(0, others * piece_rows)]
    plane_back_all = whole(back_pieces, back_pieces, plane_back_sem)
    plane_back_all.wait_recv()
    pair_back = pltpu.make_async_remote_copy(
        info_ref.at[mine_half], info_ref.at[mine_half], pair_back_sem.at[0], pair_back_sem.at[1],
        device_id=partner, device_id_type=MESH,
    )
    pair_back.start()
    send_next(PACE)
    sort_group(7)
    pair.wait_send()
    pair_back.wait_recv()
    send_next(-sent[0] % per_group)

    @pl.loop(sent[0] // per_group, groups - 1)
    def _(g):
        send(g)

    send_slots((groups - 1) * per_group, groups * per_group)

    gram_ref[...] = prior_gram_ref[...] + info_ref[...] / jnp.float32(total_rows)
    factor_and_invert(gram_ref, factor_ref, inv_ref)
    inv_high_ref[...], inv_low_ref[...] = split(inv_ref[...])

    @pl.loop(0, groups)
    def _(g):
        own = is_own(g, per_group - 1)

        @pl.when(own)
        def _():
            blocks_copy(g, 0, per_group - 1).wait_recv()

        @pl.when(jnp.logical_not(own))
        def _():
            blocks_copy(g, 0, per_group).wait_recv()

        part = pl.ds(pl.multiple_of(g * chunk, chunk), chunk)
        high, low = split(recv_ref[part, :])
        inv_high, inv_low = inv_high_ref[...], inv_low_ref[...]
        cross = ((1,), (1,))
        white = dot(high, inv_high, cross) + dot(high, inv_low, cross) + dot(low, inv_high, cross)
        for j in range(per_group):
            dz, dx, dc = offsets(g, j)
            source = row_index(NZ - dz, NX - dx, NC - dc)
            spot = pl.ds(pl.multiple_of(source * block, block), block)
            out_ref[spot, :] = white[j * block : (j + 1) * block]

    blocks_copy(0, 0, groups * per_group - 1).wait_send()
    for copy in (plane_all, line_all, back_all, plane_back_all, pair_back):
        copy.wait_send()


def copy_out(white_ref, factor_ref, white_out, factor_out, sem):
    copies = [
        pltpu.make_async_copy(white_ref, white_out, sem.at[0]),
        pltpu.make_async_copy(factor_ref, factor_out, sem.at[1]),
    ]
    for copy in copies:
        copy.start()
    for copy in copies:
        copy.wait()


def shards(observations, sensor_ids, sensor_sigma, buckets, prior_factor):
    rows_dev, state = observations.shape
    total_rows = rows_dev * lax.axis_size(("rows", "grp"))
    vmem = pl.BlockSpec(memory_space=pltpu.VMEM)
    half = state // NC
    piece = half // (NX * NY)
    dma = pltpu.SemaphoreType.DMA
    whitened, factor = pl.pallas_call(
        functools.partial(kernel, total_rows),
        out_shape=(pltpu.VMEM((rows_dev, state), F32), pltpu.VMEM((state, state), F32)),
        in_specs=[pl.BlockSpec(memory_space=pltpu.HBM)] * 5,
        out_specs=(vmem, vmem),
        scratch_shapes=[
            pltpu.VMEM((rows_dev // 128, 128), I32),
            pltpu.VMEM((1, sensor_sigma.shape[0]), F32),
            pltpu.VMEM((rows_dev // 128, 128), I32),
            pltpu.VMEM((state, state), F32),
            pltpu.VMEM((rows_dev, state), F32),
            pltpu.VMEM((rows_dev, state), BF16),
            pltpu.VMEM((rows_dev, state), BF16),
            pltpu.VMEM((rows_dev // (NX * NC), rows_dev), BF16),
            pltpu.VMEM((8, rows_dev), I32),
            pltpu.VMEM((rows_dev, 128), F32),
            pltpu.VMEM((rows_dev, state), F32),
            pltpu.VMEM((rows_dev, state), F32),
            pltpu.VMEM((state, state), F32),
            pltpu.VMEM((half, state), F32),
            pltpu.VMEM((half, state), F32),
            pltpu.VMEM((NX * NY - 1, piece, state), F32),
            pltpu.VMEM((NZ, 8, 128), F32),
            pltpu.VMEM((NZ - 1, 8, 128), F32),
            pltpu.VMEM((NZ, 8, 128), F32),
            pltpu.VMEM((state, state), F32),
            pltpu.VMEM((state, state), F32),
            pltpu.VMEM((state, state), F32),
            pltpu.VMEM((state, state), BF16),
            pltpu.VMEM((state, state), BF16),
            dma((4,)),
            dma((NX * NC // 2,)),
            dma((1,)),
            dma((NX * NC,)),
            dma((2,)),
            dma((2,)),
            dma((2,)),
            dma((2,)),
            dma((2,)),
            dma((2,)),
        ],
        compiler_params=pltpu.CompilerParams(
            collective_id=0, has_side_effects=True, vmem_limit_bytes=34 << 20
        ),
    )(
        *(
            pltpu.with_memory_space_constraint(array, pltpu.HBM)
            for array in (
                observations,
                sensor_ids.reshape(-1, 128),
                sensor_sigma.reshape(1, -1),
                buckets.reshape(-1, 128),
                prior_factor,
            )
        )
    )
    return pl.pallas_call(
        copy_out,
        out_shape=(
            jax.ShapeDtypeStruct((rows_dev, state), F32),
            jax.ShapeDtypeStruct((state, state), F32),
        ),
        in_specs=[pl.BlockSpec(memory_space=pl.ANY)] * 2,
        out_specs=(pl.BlockSpec(memory_space=pl.ANY),) * 2,
        scratch_shapes=[dma((2,))],
        compiler_params=pltpu.CompilerParams(vmem_limit_bytes=1 << 20),
    )(*(pltpu.with_memory_space_constraint(array, pltpu.VMEM) for array in (whitened, factor)))


def solution(mesh):
    in_specs = (P(("rows", "grp"), None), P(("rows", "grp")), P(), P(("rows", "grp")), P())
    out_specs = (P(("rows", "grp"), None), P())
    return jax.shard_map(shards, mesh=mesh, in_specs=in_specs, out_specs=out_specs, check_vma=False)
```

```python
import functools

import jax
import jax.numpy as jnp
from jax import lax
from jax.experimental import pallas as pl
from jax.experimental.pallas import tpu as pltpu
from jax.sharding import PartitionSpec as P

MESH = pl.DeviceIdType.MESH
F32, BF16, I32 = jnp.float32, jnp.bfloat16, jnp.int32
NZ, NX, NC, NY = 8, 4, 2, 4
STEPS = (4, 1, 7, 3, 5, 2, 6, 0)
PANEL = 128
PACE = 7


def iota(shape, dim):
    return lax.broadcasted_iota(I32, shape, dim)


def split(values):
    high = values.astype(BF16)
    return high, (values - high.astype(F32)).astype(BF16)


def dot(left, right, dims=((1,), (0,))):
    return lax.dot_general(left, right, (dims, ((), ())), preferred_element_type=F32)


def exact_dot(left, right, dims=((1,), (0,))):
    return lax.dot_general(
        left, right, (dims, ((), ())), precision=lax.Precision.HIGHEST, preferred_element_type=F32
    )


def along(piece):
    return jnp.broadcast_to(piece, (8, PANEL))


def root_of(value):
    root = lax.rsqrt(value)
    return root, root * root


def inverse_panel(block):
    tiles = PANEL // 8
    lane, sub = iota((8, PANEL), 1), iota((8, PANEL), 0)
    zero = jnp.float32(0.0)
    rows = [block[8 * q : 8 * q + 8] for q in range(tiles)]
    invs = [jnp.where(lane == sub + 8 * q, jnp.float32(1.0), zero) for q in range(tiles)]
    outs = []
    for p in range(tiles):
        scale = jnp.zeros((8, PANEL), F32)
        for k in (0, 4):
            cols = {
                q: [along(rows[q][:, 8 * p + k + n : 8 * p + k + n + 1]) for n in range(4)] for q in range(p, tiles)
            }
            m = [[along(cols[p][n][k + i : k + i + 1]) for n in range(4)] for i in range(4)]
            a, b, d = m[0][0], m[1][0], m[1][1]
            det = a * d - b * b
            root_a, inv_a = root_of(a)
            root_det, inv_det = root_of(det)
            b02, b03, b12, b13 = m[2][0], m[3][0], m[2][1], m[3][1]
            g02, g12 = (d * b02 - b * b12) * inv_det, (a * b12 - b * b02) * inv_det
            g03, g13 = (d * b03 - b * b13) * inv_det, (a * b13 - b * b03) * inv_det
            s22 = m[2][2] - b02 * g02 - b12 * g12
            s32 = m[3][2] - b03 * g02 - b13 * g12
            s33 = m[3][3] - b03 * g03 - b13 * g13
            low_det = s22 * s33 - s32 * s32
            root_s, inv_s = root_of(s22)
            root_low, inv_low = root_of(low_det)
            f, h = b * inv_a, s32 * inv_s
            for i, root in enumerate((root_a, root_det * (a * root_a), root_s, root_low * (s22 * root_s))):
                scale = jnp.where(sub == k + i, root, scale)

            def eliminate(t0, t1, t2, t3):
                t2 = t2 - g02 * t0 - g12 * t1
                t3 = t3 - g03 * t0 - g13 * t1
                return t0, t1 - f * t0, t2, t3 - h * t2

            weights = (inv_a, a * inv_det, inv_s, s22 * inv_low)
            pivot_rows = eliminate(*(along(rows[p][k + i : k + i + 1]) for i in range(4)))
            pivot_invs = eliminate(*(along(invs[p][k + i : k + i + 1]) for i in range(4)))
            pivot_rows = [value * w for value, w in zip(pivot_rows, weights)]
            pivot_invs = [value * w for value, w in zip(pivot_invs, weights)]
            for q in range(p, tiles):
                x = eliminate(*cols[q])
                if q == p:
                    x = [jnp.where(sub > k + i, x[i], zero) for i in range(4)]
                for held, pivots in ((rows, pivot_rows), (invs, pivot_invs)):
                    held[q] = held[q] - (
                        (x[0] * pivots[0] + x[1] * pivots[1]) + (x[2] * pivots[2] + x[3] * pivots[3])
                    )
        outs.append(invs[p] * scale)
    return jnp.concatenate(outs, axis=0)


def factor_and_invert(matrix_ref, factor_ref, inv_ref):
    state = matrix_ref.shape[0]
    panels = state // PANEL
    factor_ref[...] = jnp.zeros_like(factor_ref)
    down = ((0,), (0,))

    @pl.loop(0, panels)
    def _(k):
        part = pl.ds(pl.multiple_of(k * PANEL, PANEL), PANEL)
        inverse = inverse_panel(matrix_ref[part, part])
        for s in range(panels):

            @pl.when(k == s)
            def _():
                first, last = s * PANEL, (s + 1) * PANEL
                own = slice(first, last)
                wide = exact_dot(inverse, matrix_ref[own, first:])
                keep = iota((PANEL, PANEL), 1) >= iota((PANEL, PANEL), 0)
                factor_ref[own, own] = jnp.where(keep, wide[:, :PANEL], jnp.float32(0.0))
                inv_ref[own, own] = inverse
                if s:
                    inv_ref[own, :first] = exact_dot(inverse, inv_ref[own, :first])
                if s < panels - 1:
                    rest = wide[:, PANEL:]
                    factor_ref[own, last:] = rest
                    inv_ref[own, last:] = jnp.zeros((PANEL, state - last), F32)
                    matrix_ref[last:, last:] = matrix_ref[last:, last:] - exact_dot(rest, rest, down)
                    delta = exact_dot(rest, inv_ref[own, :last], down)
                    if s:
                        inv_ref[last:, :first] = inv_ref[last:, :first] - delta[:, :first]
                    inv_ref[last:, own] = -delta[:, first:]


def kernel(
    total_rows,
    x_hbm, ids_hbm, sigma_hbm, buckets_hbm, prior_hbm,
    out_ref, factor_ref,
    ids_ref, sigma_ref, buckets_ref, prior_ref, x_buf, high_ref, low_ref, pick_ref, target_ref, scale_ref, sorted_ref, recv_ref,
    gram_ref, pair_ref, half_ref, plane_ref, tiles_ref, line_ref, gather_ref, info_ref, inv_ref, prior_gram_ref,
    inv_high_ref, inv_low_ref,
    small_sem, x_sem, send_sem, recv_sem, pair_sem, plane_sem, line_sem, line_back_sem, plane_back_sem, pair_back_sem,
):
    me, y = lax.axis_index("rows"), lax.axis_index("grp")
    z, x, c = me // (NX * NC), (me // NC) % NX, me % NC
    rows_dev, state = x_hbm.shape
    groups, per_group = NX * NC, NZ
    block = rows_dev // (NZ * NX * NC)
    chunk = block * per_group

    def row_index(dz, dx, dc):
        return (((z + dz) % NZ) * NX + (x + dx) % NX) * NC + (c + dc) % NC

    barrier = pltpu.get_barrier_semaphore()
    for dz in range(NZ):
        for dx in range(NX):
            for dc in range(NC):
                if (dz, dx, dc) != (0, 0, 0):
                    pl.semaphore_signal(
                        barrier, inc=1, device_id={"rows": row_index(dz, dx, dc)}, device_id_type=MESH
                    )
    for dx in range(NX):
        for dy in range(1, NY):
            peer = {"rows": row_index(0, dx, 0), "grp": (y + dy) % NY}
            pl.semaphore_signal(barrier, inc=1, device_id=peer, device_id_type=MESH)

    smalls = [
        pltpu.make_async_copy(source, target, small_sem.at[n])
        for n, (source, target) in enumerate(
            ((buckets_hbm, buckets_ref), (ids_hbm, ids_ref), (sigma_hbm, sigma_ref), (prior_hbm, prior_ref))
        )
    ]
    for copy in smalls[:3]:
        copy.start()
    def load(n):
        part = pl.ds(pl.multiple_of(n * 2 * chunk, 2 * chunk), 2 * chunk)
        return pltpu.make_async_copy(x_hbm.at[part], x_buf.at[part], x_sem.at[n])

    for n in range(groups // 2):
        load(n).start()
    smalls[3].start()

    smalls[0].wait()

    n_buckets, n_chunks = NZ * NX * NC, rows_dev // 128
    below = (iota((128, 256), 0) <= iota((128, 256), 1)) | (iota((128, 256), 1) >= 128)
    counter = jnp.where(below, jnp.float32(1.0), jnp.float32(0.0)).astype(BF16)
    bucket_no = iota((n_buckets, 128), 0)
    base = jnp.zeros((n_buckets, 128), F32)
    for q in range(n_chunks):
        match = bucket_no == buckets_ref[q : q + 1, :]
        onehot = jnp.where(match, jnp.float32(1.0), jnp.float32(0.0))
        counts = dot(onehot.astype(BF16), counter)
        rank = counts[:, :128] + base
        base = base + counts[:, 128:]
        spot = jnp.where(match, rank.astype(I32) + (bucket_no * block - 1), 0)
        target_ref[:, 128 * q : 128 * q + 128] = jnp.broadcast_to(
            jnp.sum(spot, axis=0, keepdims=True), (8, 128)
        )

    smalls[1].wait()
    smalls[2].wait()

    weights = jnp.broadcast_to(1.0 / sigma_ref[...], (128, 128)).T
    w_high, w_mid = split(weights)
    w_low = (weights - w_high.astype(F32) - w_mid.astype(F32)).astype(BF16)
    sensor_no = iota((128, 128), 0)
    for q in range(n_chunks):
        onehot = jnp.where(sensor_no == ids_ref[q : q + 1, :], jnp.float32(1.0), jnp.float32(0.0)).T.astype(BF16)
        scale_ref[128 * q : 128 * q + 128, :] = (
            dot(onehot, w_high) + dot(onehot, w_mid) + dot(onehot, w_low)
        )

    @pl.loop(0, groups)
    def _(g):
        @pl.when(g % 2 == 0)
        def _():
            load(g // 2).wait()

        part = pl.ds(pl.multiple_of(g * chunk, chunk), chunk)
        scale = scale_ref[part, :]
        for n in range(state // 128):
            cols = slice(128 * n, 128 * n + 128)
            high, low = split(x_buf[part, cols] * scale)
            high_ref[part, cols] = high
            low_ref[part, cols] = low

    def offsets(g, j):
        return STEPS[j], (g // NC + j) % NX, g % NC

    def is_own(g, j):
        dz, dx, dc = offsets(g, j)
        return (dz == 0) & (dx == 0) & (dc == 0)

    def row_copy(g, j):
        return blocks_copy(g, j, 1)

    def blocks_copy(g, j, count):
        spot = pl.ds(pl.multiple_of(g * chunk + j * block, block), count * block)
        return pltpu.make_async_remote_copy(
            sorted_ref.at[spot], recv_ref.at[spot],
            send_sem.at[0], recv_sem.at[g * 2 + j // (per_group // 2)],
            device_id={"rows": row_index(*offsets(g, j))}, device_id_type=MESH,
        )

    def sort(g, start=0, stop=NZ):
        for j in range(start, stop):
            first = row_index(*offsets(g, j)) * block
            for i in range(block // 8):
                hit = target_ref[...] == iota((8, rows_dev), 0) + (first + 8 * i)
                pick_ref[j * block + 8 * i : j * block + 8 * i + 8, :] = jnp.where(
                    hit, jnp.float32(1.0), jnp.float32(0.0)
                ).astype(BF16)
        size = (stop - start) * block
        part = pl.ds(pl.multiple_of(g * chunk + start * block, block), size)
        pick = pick_ref[start * block : stop * block, :]
        sorted_ref[part, :] = dot(pick, high_ref[...]) + dot(pick, low_ref[...])

    def send(g, first=0, last=NZ):
        for j in range(first, last):
            if STEPS[j] == 0:
                own = is_own(g, j)
                spot = pl.ds(pl.multiple_of(g * chunk + j * block, block), block)

                @pl.when(own)
                def _():
                    recv_ref[spot, :] = sorted_ref[spot, :]

                @pl.when(jnp.logical_not(own))
                def _():
                    row_copy(g, j).start()
            else:
                row_copy(g, j).start()

    def sort_group(which, start=0, stop=NZ):
        @pl.loop(which, which + 1)
        def _(g):
            sort(g, start, stop)

    def send_slots(first, last):
        while first < last:
            which, start = first // per_group, first % per_group
            stop = min(per_group, start + last - first)

            @pl.loop(which, which + 1)
            def _(g):
                send(g, start, stop)

            first += stop - start

    def send_next(count):
        send_slots(sent[0], sent[0] + count)
        sent[0] += count

    sent = [0]
    sort_group(0, 0, per_group // 2)
    pl.semaphore_wait(barrier, NZ * NX * NC - 1 + NX * (NY - 1))
    send_next(per_group // 2)
    sort_group(0, per_group // 2, per_group)
    send_next(2)

    gram_ref[...] = jnp.zeros_like(gram_ref)

    @pl.loop(0, groups // 2)
    def _(g):
        part = pl.ds(pl.multiple_of(g * 2 * chunk, 2 * chunk), 2 * chunk)
        high, low = high_ref[part, :], low_ref[part, :]
        along = ((0,), (0,))
        gram_ref[...] += dot(high, high, along) + dot(high, low, along) + dot(low, high, along)

    half_rows = state // NC
    piece_rows = half_rows // (NX * NY)
    mine_half = pl.ds(pl.multiple_of(c * half_rows, half_rows), half_rows)
    other_half = pl.ds(pl.multiple_of((1 - c) * half_rows, half_rows), half_rows)
    partner = {"rows": row_index(0, 0, 1)}
    pair = pltpu.make_async_remote_copy(
        gram_ref.at[other_half], pair_ref, pair_sem.at[0], pair_sem.at[1], device_id=partner, device_id_type=MESH
    )
    pair.start()
    send_next(per_group // 2 - 2)

    smalls[3].wait()
    prior = prior_ref[...]
    prior_gram_ref[...] = exact_dot(prior, prior, ((0,), (0,)))
    sort_group(1)
    send_next(PACE)
    sort_group(2)
    pair.wait_recv()
    half_ref[...] = gram_ref[mine_half, :] + pair_ref[...]

    def piece(px, py):
        return pl.ds(pl.multiple_of((px * NY + py) * piece_rows, piece_rows), piece_rows)

    others = NX * NY - 1

    def whole(source, target, sems):
        return pltpu.make_async_remote_copy(
            source, target, sems.at[0], sems.at[1], device_id=partner, device_id_type=MESH
        )

    plane = [(dx, dy) for dx in range(NX) for dy in range(NY) if (dx, dy) != (0, 0)]
    for n, (dx, dy) in enumerate(plane):
        px, py = (x + dx) % NX, (y + dy) % NY
        copy = pltpu.make_async_remote_copy(
            half_ref.at[piece(px, py)], plane_ref.at[n], plane_sem.at[0], plane_sem.at[1],
            device_id={"rows": row_index(0, dx, 0), "grp": py}, device_id_type=MESH,
        )
        copy.start()
    send_next(PACE)
    sort_group(3)
    plane_all = whole(half_ref.at[pl.ds(0, others * piece_rows)], plane_ref, plane_sem)
    plane_all.wait_recv()
    total = half_ref[piece(x, y), :]
    for n in range(len(plane)):
        total = total + plane_ref[n]
    for t in range(NZ):
        tiles_ref[t] = total[8 * (t // 4) : 8 * (t // 4) + 8, 128 * (t % 4) : 128 * (t % 4) + 128]
    for dz in range(1, NZ):
        copy = pltpu.make_async_remote_copy(
            tiles_ref.at[(z + dz) % NZ], line_ref.at[dz - 1], line_sem.at[0], line_sem.at[1],
            device_id={"rows": row_index(dz, 0, 0)}, device_id_type=MESH,
        )
        copy.start()
    send_next(PACE)
    sort_group(4)
    line_all = whole(tiles_ref.at[pl.ds(0, NZ - 1)], line_ref, line_sem)
    line_all.wait_recv()
    done = tiles_ref[z]
    for dz in range(1, NZ):
        done = done + line_ref[dz - 1]
    gather_ref[z] = done
    for dz in range(1, NZ):
        copy = pltpu.make_async_remote_copy(
            gather_ref.at[z], gather_ref.at[z], line_back_sem.at[0], line_back_sem.at[1],
            device_id={"rows": row_index(dz, 0, 0)}, device_id_type=MESH,
        )
        copy.start()
    send_next(PACE)
    sort_group(5)
    back_tiles = gather_ref.at[pl.ds(0, NZ - 1)]
    back_all = whole(back_tiles, back_tiles, line_back_sem)
    back_all.wait_recv()
    own_piece = pl.ds(
        pl.multiple_of(c * half_rows + (x * NY + y) * piece_rows, piece_rows), piece_rows
    )
    info_ref[own_piece, :] = jnp.concatenate(
        [jnp.concatenate([gather_ref[4 * a + b] for b in range(4)], axis=1) for a in range(2)], axis=0
    )
    for n, (dx, dy) in enumerate(plane):
        copy = pltpu.make_async_remote_copy(
            info_ref.at[own_piece], info_ref.at[own_piece], plane_back_sem.at[0], plane_back_sem.at[1],
            device_id={"rows": row_index(0, dx, 0), "grp": (y + dy) % NY}, device_id_type=MESH,
        )
        copy.start()
    send_next(PACE)
    sort_group(6)
    back_pieces = info_ref.at[pl.ds(0, others * piece_rows)]
    plane_back_all = whole(back_pieces, back_pieces, plane_back_sem)
    plane_back_all.wait_recv()
    pair_back = pltpu.make_async_remote_copy(
        info_ref.at[mine_half], info_ref.at[mine_half], pair_back_sem.at[0], pair_back_sem.at[1],
        device_id=partner, device_id_type=MESH,
    )
    pair_back.start()
    send_next(PACE)
    sort_group(7)
    pair.wait_send()
    pair_back.wait_recv()
    send_next(-sent[0] % per_group)

    @pl.loop(sent[0] // per_group, groups - 1)
    def _(g):
        send(g)

    send_slots((groups - 1) * per_group, groups * per_group)

    gram_ref[...] = prior_gram_ref[...] + info_ref[...] / jnp.float32(total_rows)
    factor_and_invert(gram_ref, factor_ref, inv_ref)
    inv_high_ref[...], inv_low_ref[...] = split(inv_ref[...])

    @pl.loop(0, groups)
    def _(g):
        for start in (0, per_group // 2):
            count = per_group // 2
            if start:
                own = is_own(g, per_group - 1)

                @pl.when(own)
                def _():
                    blocks_copy(g, start, count - 1).wait_recv()

                @pl.when(jnp.logical_not(own))
                def _():
                    blocks_copy(g, start, count).wait_recv()
            else:
                blocks_copy(g, start, count).wait_recv()
            part = pl.ds(pl.multiple_of(g * chunk + start * block, block), count * block)
            high, low = split(recv_ref[part, :])
            inv_high, inv_low = inv_high_ref[...], inv_low_ref[...]
            cross = ((1,), (1,))
            white = dot(high, inv_high, cross) + dot(high, inv_low, cross) + dot(low, inv_high, cross)
            for j in range(count):
                dz, dx, dc = offsets(g, start + j)
                source = row_index(NZ - dz, NX - dx, NC - dc)
                spot = pl.ds(pl.multiple_of(source * block, block), block)
                out_ref[spot, :] = white[j * block : (j + 1) * block]

    blocks_copy(0, 0, groups * per_group - 1).wait_send()
    for copy in (plane_all, line_all, back_all, plane_back_all, pair_back):
        copy.wait_send()


def copy_out(white_ref, factor_ref, white_out, factor_out, sem):
    copies = [
        pltpu.make_async_copy(white_ref, white_out, sem.at[0]),
        pltpu.make_async_copy(factor_ref, factor_out, sem.at[1]),
    ]
    for copy in copies:
        copy.start()
    for copy in copies:
        copy.wait()


def shards(observations, sensor_ids, sensor_sigma, buckets, prior_factor):
    rows_dev, state = observations.shape
    total_rows = rows_dev * lax.axis_size(("rows", "grp"))
    vmem = pl.BlockSpec(memory_space=pltpu.VMEM)
    half = state // NC
    piece = half // (NX * NY)
    dma = pltpu.SemaphoreType.DMA
    whitened, factor = pl.pallas_call(
        functools.partial(kernel, total_rows),
        out_shape=(pltpu.VMEM((rows_dev, state), F32), pltpu.VMEM((state, state), F32)),
        in_specs=[pl.BlockSpec(memory_space=pltpu.HBM)] * 5,
        out_specs=(vmem, vmem),
        scratch_shapes=[
            pltpu.VMEM((rows_dev // 128, 128), I32),
            pltpu.VMEM((1, sensor_sigma.shape[0]), F32),
            pltpu.VMEM((rows_dev // 128, 128), I32),
            pltpu.VMEM((state, state), F32),
            pltpu.VMEM((rows_dev, state), F32),
            pltpu.VMEM((rows_dev, state), BF16),
            pltpu.VMEM((rows_dev, state), BF16),
            pltpu.VMEM((rows_dev // (NX * NC), rows_dev), BF16),
            pltpu.VMEM((8, rows_dev), I32),
            pltpu.VMEM((rows_dev, 128), F32),
            pltpu.VMEM((rows_dev, state), F32),
            pltpu.VMEM((rows_dev, state), F32),
            pltpu.VMEM((state, state), F32),
            pltpu.VMEM((half, state), F32),
            pltpu.VMEM((half, state), F32),
            pltpu.VMEM((NX * NY - 1, piece, state), F32),
            pltpu.VMEM((NZ, 8, 128), F32),
            pltpu.VMEM((NZ - 1, 8, 128), F32),
            pltpu.VMEM((NZ, 8, 128), F32),
            pltpu.VMEM((state, state), F32),
            pltpu.VMEM((state, state), F32),
            pltpu.VMEM((state, state), F32),
            pltpu.VMEM((state, state), BF16),
            pltpu.VMEM((state, state), BF16),
            dma((4,)),
            dma((NX * NC // 2,)),
            dma((1,)),
            dma((2 * NX * NC,)),
            dma((2,)),
            dma((2,)),
            dma((2,)),
            dma((2,)),
            dma((2,)),
            dma((2,)),
        ],
        compiler_params=pltpu.CompilerParams(
            collective_id=0, has_side_effects=True, vmem_limit_bytes=34 << 20
        ),
    )(
        *(
            pltpu.with_memory_space_constraint(array, pltpu.HBM)
            for array in (
                observations,
                sensor_ids.reshape(-1, 128),
                sensor_sigma.reshape(1, -1),
                buckets.reshape(-1, 128),
                prior_factor,
            )
        )
    )
    return pl.pallas_call(
        copy_out,
        out_shape=(
            jax.ShapeDtypeStruct((rows_dev, state), F32),
            jax.ShapeDtypeStruct((state, state), F32),
        ),
        in_specs=[pl.BlockSpec(memory_space=pl.ANY)] * 2,
        out_specs=(pl.BlockSpec(memory_space=pl.ANY),) * 2,
        scratch_shapes=[dma((2,))],
        compiler_params=pltpu.CompilerParams(vmem_limit_bytes=1 << 20),
    )(*(pltpu.with_memory_space_constraint(array, pltpu.VMEM) for array in (whitened, factor)))


def solution(mesh):
    in_specs = (P(("rows", "grp"), None), P(("rows", "grp")), P(), P(("rows", "grp")), P())
    out_specs = (P(("rows", "grp"), None), P())
    return jax.shard_map(shards, mesh=mesh, in_specs=in_specs, out_specs=out_specs, check_vma=False)
```
